128 devices in a mesh: line: 8 (over y, core), bus: 16 (over x, z).
Axes of the slice: x: 4, y: 4, z: 4, core: 2. Of those that a mesh axis runs over, the one named last changes fastest.
Arguments:
- site_values: float32 [512, 65536], P('line', 'bus'), may hold values from -6 to 6
- site_bus: int32 [65536], replicated, may hold values from 0 to 71679, as said below
- block_count: int32 [88, 16], P('line', 'bus'), may hold values from 0 to 3
- block_zone: int32 [88, 48], P('line', 'bus'), may hold values from 0 to 6, as said below
- ptdf_blocks: bfloat16 [88, 48, 512, 640], P('line', 'bus'), may hold values from -0.0625 to 0.0625
- rating: float32 [45056], P('line'), may hold values from 0.5 to 4
Outputs:
- loading: float32 [512, 45056], P('bus', 'line')
- worst: float32 [45056], P('line')
The draws below stay inside these ranges and needn't reach their ends.
Inputs may be any that keep to these rules, and one draw needn't show every extreme that they name: `site_bus`: every aligned block of 4096 sites holds exactly 256 sites whose bus lies in each bus group, the range of 4480 consecutive buses; bus 0 and the last bus each carry a site. `block_zone`: for each line zone, the 3 slots of one bus group name distinct zones of that group.
All inputs are finite; a program needn't handle non-finite values.
Results may differ from the reference program's by a relative error of at most 0.015.
Values may be sent and summed in bfloat16 or wider, within the bound.
A program may use at most 128 MiB of HBM per device.

```python
import math
import jax
import jax.numpy as jnp
from jax import lax

NB = 71680
NL = 45056
ZL = 512
ZB = 640
CAP = 3
SCEN = 512
SITE_DEV = 4096
LZ = 88
BZ = 112
BZD = 7
BUS_DEV = 4480
SITES = 65536
N_BUS = 16


def draw_site_bus(key, part):
    group_total = SITES // SITE_DEV
    first, second = jax.random.split(jax.random.fold_in(key, 11), 2)
    base = jnp.repeat(jnp.arange(group_total, dtype=jnp.int32), SITE_DEV // group_total)
    block_keys = jax.random.split(first, group_total)
    shuffled = jax.vmap(lambda k: jax.random.permutation(k, base))(block_keys)
    offset = jax.random.randint(second, (group_total, SITE_DEV), 0, BUS_DEV, dtype=jnp.int32)
    flat = (shuffled * BUS_DEV + offset).reshape(SITES).astype(jnp.int32)
    groups = flat // BUS_DEV
    high_pos = jnp.argmax(groups == group_total - 1)
    low_pos = jnp.argmax(groups == 0)
    flat = flat.at[high_pos].set(NB - 1)
    flat = flat.at[low_pos].set(0)
    return flat.astype(jnp.int32)


def draw_block_zone(key, part):
    group_total = NB // BUS_DEV
    keys = jax.random.split(jax.random.fold_in(key, 23), LZ * group_total)
    picks = jax.vmap(lambda k: jax.random.permutation(k, BZD)[:CAP])(keys)
    return picks.reshape(LZ, group_total * CAP).astype(jnp.int32)


def touch_ends(result, own_key, smallest, top_value):
    index_at = [jax.random.randint(jax.random.fold_in(own_key, axis), (), 0, length) for axis, length in enumerate(result.shape)]
    widest = result.shape.index(max(result.shape))
    next_to = index_at[:widest] + [(index_at[widest] + 1) % result.shape[widest]] + index_at[widest + 1:]
    return result.at[tuple(index_at)].set(smallest).at[tuple(next_to)].set(top_value)


def block_levels(own_key, extent, pieces, smallest, top_value):
    def one(axis_at, blocks):
        heights = jax.random.uniform(jax.random.fold_in(jax.random.fold_in(own_key, 6), axis_at), (blocks,), jnp.float32, smallest / len(pieces), top_value / len(pieces))
        return jnp.repeat(jnp.exp(heights), extent[axis_at] // blocks).reshape((-1,) + (1,) * (len(extent) - axis_at - 1))

    gain = one(*pieces[0])
    for cut in pieces[1:]:
        gain = gain * one(*cut)
    return gain


def noise(rng, shape, deviation, bound, cuts=(), kind=jnp.bfloat16):
    drawn = jax.random.normal(rng, shape, jnp.float32) * deviation
    if len(cuts) > 0:
        drawn = block_levels(rng, shape, cuts, -0.22, 0.18) * drawn
    return jnp.clip(drawn, min=-bound, max=bound).astype(kind)


def setup_inputs(seed: int = 0) -> dict:
    key_list = jax.random.split(jax.random.key(seed), 7)
    return {
        "site_values": noise(key_list[0], (SCEN, SITES), 1.0, 6.0, ((0, 8), (1, 16)), jnp.float32),
        "site_bus": draw_site_bus(jax.random.fold_in(key_list[6], 71), 0),
        "block_count": touch_ends(jax.random.randint(key_list[2], (LZ, N_BUS), 0, CAP + 1), jax.random.fold_in(key_list[2], 1), 0, CAP).astype(jnp.int32),
        "block_zone": draw_block_zone(jax.random.fold_in(key_list[6], 71), 0),
        "ptdf_blocks": noise(key_list[4], (LZ, N_BUS * CAP, ZL, ZB), (ZB * N_BUS) ** -0.5, 0.0625, ((0, 8), (1, 16))),
        "rating": jnp.clip(jnp.exp(math.log(4.0) - 2.0794415 * jax.random.uniform(key_list[5], (NL,), jnp.float32) ** block_levels(key_list[5], (NL,), ((0, 8),), -0.2, 0.2)), 0.5, 4.0),
    }


def reference(site_values, site_bus, block_count, block_zone, ptdf_blocks, rating):
    summed = jnp.zeros((SCEN, NB), jnp.float32).at[:, site_bus].add(site_values.astype(jnp.float32))
    injection = summed.astype(jnp.bfloat16)
    inj_zones = injection.astype(jnp.float32).reshape(SCEN, BZ, ZB)
    slot_ids = jnp.arange(N_BUS * CAP).astype(jnp.int32)
    offsets = ((slot_ids // CAP) * BZD).astype(jnp.int32)

    def one_zone(carry, inputs):
        counts, zones, blocks = inputs
        global_zone = (offsets + zones).astype(jnp.int32)
        live = ((slot_ids % CAP) < jnp.repeat(counts, CAP)).astype(jnp.float32).reshape(N_BUS, CAP)
        picked = jnp.take(inj_zones, global_zone, axis=1).reshape(SCEN, N_BUS, CAP, ZB)
        grouped = blocks.astype(jnp.float32).reshape(N_BUS, CAP, ZL, ZB)
        parts = jnp.einsum("sgcb,gclb,gc->sgl", picked, grouped, live)
        rounded = lax.optimization_barrier(parts.astype(jnp.bfloat16))
        flow = jnp.sum(rounded.astype(jnp.float32), axis=1)
        return carry, flow

    _, flows = lax.scan(one_zone, jnp.float32(0.0), (block_count, block_zone, ptdf_blocks))
    flow = jnp.transpose(flows, (1, 0, 2)).reshape(SCEN, NL)
    loading = flow / rating[None, :]
    worst = jnp.max(jnp.abs(loading), axis=0)
    return loading, worst
```

```python
import functools

import jax
import jax.numpy as jnp
from jax import lax
from jax.experimental import pallas as pl
from jax.experimental.pallas import tpu as pltpu
from jax.sharding import PartitionSpec as P

MESH = pl.DeviceIdType.MESH
F32 = jnp.float32
BF16 = jnp.bfloat16

LINES = 8
BUSES = 16
RING = 4
BUS_DEV = 4480
SCEN_DEV = 64
SITE_DEV = 4096
PER = 256
ROWS = 80
CHUNKS = SITE_DEV // 128
ZONES = 7
ZB = 640
LZ = 11
ZL = 512
SLOTS = 3
HALF = 256
T = 2 * LZ
NT = (((1,), (1,)), ((), ()))
LAG = (2, 4, 6, 8)
WSPLIT = 8


def iota(shape, dim):
    return lax.broadcasted_iota(jnp.int32, shape, dim).astype(F32)


def kernel(
    count_ref, zone_ref, values_hbm, bus_hbm, blocks_hbm, rating_ref,
    load_ref, worst_ref,
    ids, grp, hi, lo, xa, g01, pre, bt, lhs, sv, rv, blk, inj0, inj1,
    flows, ra, rb, sa, rc, rd, wl, wr,
    in_sem, blk_sem, xs_sem, xr_sem, gs_sem, gr_sem, fs_sem, fr_sem, ws_sem, wr_sem,
):
    line = lax.axis_index("line")
    bus = lax.axis_index("bus")
    y, core = line // 2, line % 2
    x, z = bus // RING, bus % RING
    up = ((y + 1) % RING) * 2 + core
    down = ((y + 3) % RING) * 2 + core
    sib = y * 2 + (1 - core)
    x1, x2, x3 = (x + 1) % RING, (x + 2) % RING, (x + 3) % RING
    z1, z2, z3 = (z + 1) % RING, (z + 2) % RING, (z + 3) % RING

    ids_copy = pltpu.make_async_copy(bus_hbm.at[pl.ds(bus * CHUNKS, CHUNKS)], ids, in_sem.at[0])
    ids_copy.start()
    val_copy = pltpu.make_async_copy(values_hbm, xa.at[pl.ds(0, SCEN_DEV)], in_sem.at[1])
    val_copy.start()

    barrier = pltpu.get_barrier_semaphore()
    for j in range(1, BUSES):
        pl.semaphore_signal(barrier, inc=1, device_id=(line, (bus + j) % BUSES), device_id_type=MESH)
    for other in (up, down, sib):
        pl.semaphore_signal(barrier, inc=1, device_id=(other, bus), device_id_type=MESH)

    def block_copy(zone, slot):
        return pltpu.make_async_copy(
            blocks_hbm.at[zone, slot], blk.at[zone, :, pl.ds(slot * ZB, ZB)], blk_sem.at[zone, slot]
        )

    def start_blocks(zone, _):
        for slot in range(SLOTS):
            block_copy(zone, slot).start()
        return 0

    lax.fori_loop(0, LZ, start_blocks, 0)

    inj0[ZONES] = jnp.zeros((HALF, ZB), BF16)
    inj1[ZONES] = jnp.zeros((HALF, ZB), BF16)
    wl[...] = jnp.zeros_like(wl)
    ids_copy.wait()
    bus_ids = ids[...]
    group = jnp.zeros_like(bus_ids)
    for g in range(1, BUSES):
        group = group + (bus_ids >= g * BUS_DEV).astype(jnp.int32)
    offset = bus_ids - group * BUS_DEV
    grp[...] = group.astype(F32)
    hi[...] = (offset >> 8).astype(F32)
    lo[...] = (offset & 255).astype(F32)

    sub16 = iota((16, 128), 0)

    def lanes(c, width=128):
        return pl.ds(pl.multiple_of(c * width, width), width)

    def mark(c, _):
        row = grp[pl.ds(c, 1), :]
        g01[pl.ds(pl.multiple_of(c * 16, 16), 16), :] = jnp.where(row == sub16, 1.0, 0.0).astype(BF16)
        digits = jnp.where(sub16 == 0, hi[pl.ds(c, 1), :], jnp.where(sub16 == 1, lo[pl.ds(c, 1), :], 0.0))
        xa[pl.ds(SCEN_DEV, 16), lanes(c)] = digits
        return 0

    lax.fori_loop(0, CHUNKS, mark, 0)
    ahead = lax.broadcasted_iota(jnp.int32, (128, 256), 0)
    place = lax.broadcasted_iota(jnp.int32, (128, 256), 1)
    steps = jnp.where((ahead <= place) | (place >= 128), 1.0, 0.0).astype(BF16)
    pre[...] = jnp.dot(g01[...], steps, preferred_element_type=F32)
    sub256 = iota((256, 128), 0)

    def rank(c, run):
        rows = pl.ds(pl.multiple_of(c * 16, 16), 16)
        counted = g01[rows, :].astype(F32) * (pre[rows, pl.ds(0, 128)] + run)
        position = jnp.sum(counted, axis=0, keepdims=True) - 1.0
        bt[:, lanes(c)] = jnp.where(position == sub256, 1.0, 0.0).astype(BF16)
        return run + pre[rows, pl.ds(128, 128)]

    lax.fori_loop(0, CHUNKS, rank, jnp.zeros((16, 128), F32))
    val_copy.wait()

    def exchange(j, owner):
        return pltpu.make_async_remote_copy(
            sv.at[j], rv.at[bus], xs_sem.at[j], xr_sem.at[bus],
            device_id=(line, owner), device_id_type=MESH,
        )

    pl.semaphore_wait(barrier, BUSES - 1 + 3)
    for batch in range(4):
        owners = [(bus + batch * 4 + i + 1) % BUSES for i in range(4)]
        owners_f = [o.astype(F32) for o in owners]

        def pick(c, _):
            row = grp[pl.ds(c, 1), :]
            vals = xa[:, lanes(c)]
            for i in range(4):
                lhs[pl.ds(i * ROWS, ROWS), lanes(c)] = jnp.where(row == owners_f[i], vals, 0.0).astype(BF16)
            return 0

        lax.fori_loop(0, CHUNKS, pick, 0)
        packed = lax.dot_general(
            lhs[pl.ds(0, 4 * ROWS), :], bt[...], NT, preferred_element_type=F32
        ).astype(BF16)
        for i in range(4):
            j = batch * 4 + i
            if j < BUSES - 1:
                sv[j] = packed[i * ROWS:(i + 1) * ROWS]
                exchange(j, owners[i]).start()
            else:
                rv[bus] = packed[i * ROWS:(i + 1) * ROWS]

    for j in range(1, BUSES):
        src = (bus + j) % BUSES
        pltpu.make_async_copy(rv.at[src], rv.at[src], xr_sem.at[src]).wait()

    sub256w = iota((256, 256), 0)

    def low_digit(k, _):
        row = rv[k, pl.ds(SCEN_DEV, 16), :].astype(F32)[1:2]
        bt[:, lanes(k, 256)] = jnp.where(row == sub256w, 1.0, 0.0).astype(BF16)
        return 0

    lax.fori_loop(0, BUSES, low_digit, 0)
    for part in range(3):

        def high_digit(k, _):
            vals = rv[k, pl.ds(0, SCEN_DEV), :].astype(F32)
            row = rv[k, pl.ds(SCEN_DEV, 16), :].astype(F32)[0:1]
            for i in range(6):
                lhs[pl.ds(i * SCEN_DEV, SCEN_DEV), lanes(k, 256)] = jnp.where(
                    row == float(part * 6 + i), vals, 0.0
                ).astype(BF16)
            return 0

        lax.fori_loop(0, BUSES, high_digit, 0)
        spread = lax.dot_general(
            lhs[...], bt[...], NT, preferred_element_type=F32
        ).astype(BF16)
        for i in range(6):
            for t in range(2):
                strip = 2 * (part * 6 + i) + t
                if strip >= ZONES * 5:
                    continue
                zone, lane = strip // 5, (strip % 5) * 128
                for s in range(4):
                    half, row = s % 2, (s // 2) * 16
                    dst = inj1 if half else inj0
                    dst[zone, pl.ds(pl.multiple_of(line * 32, 32) + row, 16), lane:lane + 128] = spread[
                        i * SCEN_DEV + s * 16:i * SCEN_DEV + s * 16 + 16, t * 128:t * 128 + 128
                    ]

    def gather(half, number, owner, first, count, target):
        buf = inj1 if half else inj0
        rows = buf.at[pl.ds(0, ZONES), pl.ds(pl.multiple_of(owner * 32, 32) + first, count)]
        return pltpu.make_async_remote_copy(
            rows, rows, gs_sem.at[half, number], gr_sem.at[half, number],
            device_id=(target, bus), device_id_type=MESH,
        )

    def arrival(half, number, owner, first, count):
        buf = inj1 if half else inj0
        rows = buf.at[pl.ds(0, ZONES), pl.ds(pl.multiple_of(owner * 32, 32) + first, count)]
        return pltpu.make_async_copy(rows, rows, gr_sem.at[half, number])

    far = ((y + 2) % RING) * 2 + core
    sib_up = ((y + 1) % RING) * 2 + (1 - core)
    sib_down = ((y + 3) % RING) * 2 + (1 - core)
    sib_far = ((y + 2) % RING) * 2 + (1 - core)

    ROUTES = (
        (line, 0, 32, up),
        (line, 0, 32, down),
        (line, 0, 32, sib),
        (down, 0, 16, up),
        (down, 0, 32, sib),
        (up, 16, 16, down),
        (up, 0, 32, sib),
        (far, 0, 16, sib),
        (far, 16, 16, sib),
    )

    def route(half, number):
        return gather(half, number, *ROUTES[number])

    def gather_start(half):
        for number in range(3):
            route(half, number).start()

    def gather_relay(half):
        arrival(half, 0, down, 0, 32).wait()
        route(half, 3).start()
        route(half, 4).start()
        arrival(half, 1, up, 0, 32).wait()
        route(half, 5).start()
        route(half, 6).start()

    def gather_last(half):
        arrival(half, 3, far, 0, 16).wait()
        route(half, 7).start()
        arrival(half, 5, far, 16, 16).wait()
        route(half, 8).start()

    def gather_finish(half):
        arrival(half, 2, sib, 0, 32).wait()
        arrival(half, 4, sib_down, 0, 32).wait()
        arrival(half, 6, sib_up, 0, 32).wait()
        arrival(half, 7, sib_far, 0, 16).wait()
        arrival(half, 8, sib_far, 16, 16).wait()

    gather_start(0)
    gather_relay(0)
    gather_start(1)
    gather_last(0)
    gather_finish(0)

    A, B = pl.ds(0, 256), pl.ds(256, 256)
    L, R = pl.ds(0, 128), pl.ds(128, 128)
    LO, HI = pl.ds(0, 2), pl.ds(2, 2)
    ALL = pl.ds(0, 4)

    def push(src, dst, t, step, device):
        pltpu.make_async_remote_copy(
            src, dst, fs_sem.at[t, step], fr_sem.at[t, step],
            device_id=(line, device), device_id_type=MESH,
        ).start()

    xp, xm, zp, zm = x1 * RING + z, x3 * RING + z, x * RING + z1, x * RING + z3

    def produce(t, zone, inj):
        for slot in range(SLOTS):
            @pl.when(t < LZ)
            def _():
                block_copy(zone, slot).wait()
        live = count_ref[zone, 0]
        pieces = []
        for slot in range(SLOTS):
            at = jnp.where(slot < live, zone_ref[zone, slot], ZONES)
            pieces.append(inj[at])
        out = lax.dot_general(
            jnp.concatenate(pieces, axis=1), blk[zone], NT, preferred_element_type=F32
        ).astype(BF16)
        flows[t] = out.reshape(RING, RING, 16, ZL)
        push(flows.at[t, x2, LO, :, A], ra.at[t, 0], t, 0, xp)
        push(flows.at[t, x2, HI, :, A], ra.at[t, 1], t, 0, xm)
        push(flows.at[t, LO, z2, :, B], ra.at[t, 2], t, 0, zp)
        push(flows.at[t, HI, z2, :, B], ra.at[t, 3], t, 0, zm)

    def arrived(buf, t, step):
        pltpu.make_async_copy(buf.at[t], buf.at[t], fr_sem.at[t, step]).wait()

    def add(a, b):
        return (a.astype(F32) + b.astype(F32)).astype(BF16)

    def first_b(t):
        arrived(ra, t, 0)
        flows[t, x1, LO, :, A] = add(flows[t, x1, LO, :, A], ra[t, 0])
        push(flows.at[t, x1, ALL, :, A], rb.at[t, 0], t, 1, xp)
        flows[t, x3, HI, :, A] = add(flows[t, x3, HI, :, A], ra[t, 1])
        push(flows.at[t, x3, ALL, :, A], rb.at[t, 1], t, 1, xm)
        flows[t, LO, z1, :, B] = add(flows[t, LO, z1, :, B], ra[t, 2])
        push(flows.at[t, ALL, z1, :, B], rb.at[t, 2], t, 1, zp)
        flows[t, HI, z3, :, B] = add(flows[t, HI, z3, :, B], ra[t, 3])
        push(flows.at[t, ALL, z3, :, B], rb.at[t, 3], t, 1, zm)

    def add3(a, b, c):
        return a.astype(F32) + b.astype(F32) + c.astype(F32)

    def second_a(t):
        arrived(rb, t, 1)
        sa[t, 0] = add3(flows[t, x, ALL, :, A], rb[t, 0], rb[t, 1]).astype(BF16)
        push(sa.at[t, 0, z2, :, L], rc.at[t, 0], t, 2, zp)
        push(sa.at[t, 0, z2, :, R], rc.at[t, 1], t, 2, zm)
        sa[t, 1] = add3(flows[t, ALL, z, :, B], rb[t, 2], rb[t, 3]).astype(BF16)
        push(sa.at[t, 1, x2, :, L], rc.at[t, 2], t, 2, xp)
        push(sa.at[t, 1, x2, :, R], rc.at[t, 3], t, 2, xm)

    def second_b(t):
        arrived(rc, t, 2)
        sa[t, 0, z1, :, L] = add(sa[t, 0, z1, :, L], rc[t, 0])
        push(sa.at[t, 0, z1], rd.at[t, 0], t, 3, zp)
        sa[t, 0, z3, :, R] = add(sa[t, 0, z3, :, R], rc[t, 1])
        push(sa.at[t, 0, z3], rd.at[t, 1], t, 3, zm)
        sa[t, 1, x1, :, L] = add(sa[t, 1, x1, :, L], rc[t, 2])
        push(sa.at[t, 1, x1], rd.at[t, 2], t, 3, xp)
        sa[t, 1, x3, :, R] = add(sa[t, 1, x3, :, R], rc[t, 3])
        push(sa.at[t, 1, x3], rd.at[t, 3], t, 3, xm)

    def finish(t, zone, half):
        arrived(rd, t, 3)
        ratings = jnp.concatenate([rating_ref[pl.ds(zone * 4 + i, 1), :] for i in range(4)], axis=1)
        flow = jnp.concatenate(
            [add3(sa[t, 0, z], rd[t, 0], rd[t, 1]), add3(sa[t, 1, x], rd[t, 2], rd[t, 3])], axis=1
        )
        loading = flow / ratings
        load_ref[pl.ds(pl.multiple_of(half * 16, 16), 16), lanes(zone, ZL)] = loading
        top = jnp.max(jnp.abs(loading), axis=0, keepdims=True)
        for i in range(4):
            row = pl.ds(zone * 4 + i, 1)
            wl[row, :] = jnp.maximum(wl[row, :], top[:, i * 128:(i + 1) * 128])
        for step, buf in enumerate((ra, rb, rc, rd)):
            pltpu.make_async_copy(buf.at[t], buf.at[t], fs_sem.at[t, step]).wait()

    parts = (pl.ds(0, WSPLIT * 4), pl.ds(WSPLIT * 4, 48 - WSPLIT * 4))

    def share(part):
        for j in range(1, BUSES):
            pltpu.make_async_remote_copy(
                wl.at[parts[part]], wr.at[bus, parts[part]], ws_sem.at[part, j], wr_sem.at[part, bus],
                device_id=(line, (bus + j) % BUSES), device_id_type=MESH,
            ).start()

    def stages(t):
        d1, d2, d3, d4 = LAG

        def when(lag, stage):
            @pl.when((t >= lag) & (t < T + lag))
            def _():
                stage(t - lag)

        when(d1, first_b)
        when(d2, second_a)
        when(d3, second_b)

        @pl.when((t >= d4) & (t < T + d4))
        def _():
            finish(t - d4, (t - d4) % LZ, (t - d4) // LZ)

        @pl.when(t == d4 + LZ + WSPLIT - 1)
        def _():
            share(0)

    def first_half(t, _):
        produce(t, t, inj0)

        @pl.when(t == 4)
        def _():
            gather_relay(1)

        @pl.when(t == 8)
        def _():
            gather_last(1)

        stages(t)
        return 0

    def second_half(t, _):
        produce(t, t - LZ, inj1)
        stages(t)
        return 0

    def drain(t, _):
        stages(t)
        return 0

    lax.fori_loop(0, LZ, first_half, 0)
    gather_finish(1)
    lax.fori_loop(LZ, T, second_half, 0)
    lax.fori_loop(T, T + LAG[3], drain, 0)

    share(1)
    for half in range(2):
        for number in range(len(ROUTES)):
            route(half, number).wait_send()
    for j in range(BUSES - 1):
        pltpu.make_async_copy(sv.at[j], sv.at[j], xs_sem.at[j]).wait()
    best = wl[...]
    for part in range(2):
        for j in range(1, BUSES):
            src = wr.at[(bus + j) % BUSES, parts[part]]
            pltpu.make_async_copy(src, src, wr_sem.at[part, (bus + j) % BUSES]).wait()
    for j in range(1, BUSES):
        best = jnp.maximum(best, wr[(bus + j) % BUSES])
    worst_ref[...] = best[0:LZ * 4]
    for part in range(2):
        for j in range(1, BUSES):
            src = wl.at[parts[part]]
            pltpu.make_async_copy(src, src, ws_sem.at[part, j]).wait()


def body(site_values, site_bus, block_count, block_zone, ptdf_blocks, rating):
    smem = pl.BlockSpec(memory_space=pltpu.SMEM)
    hbm = pl.BlockSpec(memory_space=pl.ANY)
    vmem = pl.BlockSpec(memory_space=pltpu.VMEM)
    dma = pltpu.SemaphoreType.DMA
    loading, worst = pl.pallas_call(
        kernel,
        out_shape=(
            jax.ShapeDtypeStruct((32, LZ * ZL), F32),
            jax.ShapeDtypeStruct((LZ * 4, 128), F32),
        ),
        in_specs=[smem, smem, hbm, hbm, hbm, vmem],
        out_specs=(vmem, vmem),
        scratch_shapes=[
            pltpu.VMEM((CHUNKS, 128), jnp.int32),
            pltpu.VMEM((CHUNKS, 128), F32),
            pltpu.VMEM((CHUNKS, 128), F32),
            pltpu.VMEM((CHUNKS, 128), F32),
            pltpu.VMEM((ROWS, SITE_DEV), F32),
            pltpu.VMEM((CHUNKS * 16, 128), BF16),
            pltpu.VMEM((CHUNKS * 16, 256), F32),
            pltpu.VMEM((256, SITE_DEV), BF16),
            pltpu.VMEM((384, SITE_DEV), BF16),
            pltpu.VMEM((BUSES - 1, ROWS, PER), BF16),
            pltpu.VMEM((BUSES, ROWS, PER), BF16),
            pltpu.VMEM((LZ, ZL, SLOTS * ZB), BF16),
            pltpu.VMEM((ZONES + 1, HALF, ZB), BF16),
            pltpu.VMEM((ZONES + 1, HALF, ZB), BF16),
            pltpu.VMEM((T, RING, RING, 16, ZL), BF16),
            pltpu.VMEM((T, 4, 2, 16, 256), BF16),
            pltpu.VMEM((T, 4, 4, 16, 256), BF16),
            pltpu.VMEM((T, 2, 4, 16, 256), BF16),
            pltpu.VMEM((T, 4, 16, 128), BF16),
            pltpu.VMEM((T, 4, 16, 256), BF16),
            pltpu.VMEM((48, 128), F32),
            pltpu.VMEM((BUSES, 48, 128), F32),
            dma((2,)),
            dma((LZ, SLOTS)),
            dma((BUSES,)),
            dma((BUSES,)),
            dma((2, 9)),
            dma((2, 9)),
            dma((T, 4)),
            dma((T, 4)),
            dma((2, BUSES)),
            dma((2, BUSES)),
        ],
        compiler_params=pltpu.CompilerParams(
            collective_id=0, has_side_effects=True, vmem_limit_bytes=62 * 1024 * 1024
        ),
        name="screen",
    )(
        block_count, block_zone, site_values, site_bus.reshape(-1, 128), ptdf_blocks,
        rating.reshape(-1, 128),
    )
    return loading, worst.reshape(-1)


def solution(mesh):
    return jax.shard_map(
        body,
        mesh=mesh,
        in_specs=(
            P("line", "bus"),
            P(),
            P("line", "bus"),
            P("line", "bus"),
            P("line", "bus", None, None),
            P("line"),
        ),
        out_specs=(P("bus", "line"), P("line")),
        check_vma=False,
    )
```

```python
import functools

import jax
import jax.numpy as jnp
from jax import lax
from jax.experimental import pallas as pl
from jax.experimental.pallas import tpu as pltpu
from jax.sharding import PartitionSpec as P

MESH = pl.DeviceIdType.MESH
F32 = jnp.float32
BF16 = jnp.bfloat16

LINES = 8
BUSES = 16
RING = 4
BUS_DEV = 4480
SCEN_DEV = 64
SITE_DEV = 4096
PER = 256
ROWS = (48, 32)
ROWS_ALL = 80
DIGITS = 32
CHUNKS = SITE_DEV // 128
ZONES = 7
ZB = 640
LZ = 11
ZL = 512
SLOTS = 3
HALF = 256
T = 2 * LZ
NT = (((1,), (1,)), ((), ()))
LAG = (4, 8, 12, 16)
WSPLIT = 8


def iota(shape, dim):
    return lax.broadcasted_iota(jnp.int32, shape, dim).astype(F32)


def kernel(
    count_hbm, zone_hbm, values_hbm, bus_hbm, blocks_hbm, rating_ref,
    load_ref, worst_ref,
    live_ref, slot_ref, ids, grp, hi, lo, raw, xa, g01, pre, bt, lhs, sv0, sv1, rv0, rv1, blk, inj0, inj1,
    flows, ra, rb, sa, rc, rd, wl, wr,
    in_sem, blk_sem, xs_sem, xr_sem, gs_sem, gr_sem, fs_sem, fr_sem, ws_sem, wr_sem,
):
    line = lax.axis_index("line")
    bus = lax.axis_index("bus")
    y, core = line // 2, line % 2
    x, z = bus // RING, bus % RING
    up = ((y + 1) % RING) * 2 + core
    down = ((y + 3) % RING) * 2 + core
    sib = y * 2 + (1 - core)
    x1, x2, x3 = (x + 1) % RING, (x + 2) % RING, (x + 3) % RING
    z1, z2, z3 = (z + 1) % RING, (z + 2) % RING, (z + 3) % RING

    ids_copy = pltpu.make_async_copy(bus_hbm.at[pl.ds(bus * CHUNKS, CHUNKS)], ids, in_sem.at[0])
    ids_copy.start()
    val_copies = [
        pltpu.make_async_copy(values_hbm.at[pl.ds(16 * q, 16)], raw.at[pl.ds(row, 16)], in_sem.at[1 + q])
        for q, row in enumerate((0, 48, 16, 64))
    ]
    for copy in val_copies:
        copy.start()
    small_copies = [
        pltpu.make_async_copy(count_hbm, live_ref, in_sem.at[5]),
        pltpu.make_async_copy(zone_hbm, slot_ref, in_sem.at[6]),
    ]
    for copy in small_copies:
        copy.start()

    barrier = pltpu.get_barrier_semaphore()
    for j in range(1, BUSES):
        pl.semaphore_signal(barrier, inc=1, device_id=(line, (bus + j) % BUSES), device_id_type=MESH)
    for other in (up, down, sib):
        pl.semaphore_signal(barrier, inc=1, device_id=(other, bus), device_id_type=MESH)

    def block_copy(zone, slot):
        return pltpu.make_async_copy(
            blocks_hbm.at[zone, slot], blk.at[zone, :, pl.ds(slot * ZB, ZB)], blk_sem.at[zone, slot]
        )

    def start_blocks(zone, _):
        for slot in range(SLOTS):
            block_copy(zone, slot).start()
        return 0

    lax.fori_loop(0, LZ, start_blocks, 0)

    inj0[ZONES] = jnp.zeros((HALF, ZB), BF16)
    inj1[ZONES] = jnp.zeros((HALF, ZB), BF16)
    wl[...] = jnp.zeros_like(wl)
    ids_copy.wait()
    bus_ids = ids[...]
    group = jnp.zeros_like(bus_ids)
    for g in range(1, BUSES):
        group = group + (bus_ids >= g * BUS_DEV).astype(jnp.int32)
    offset = bus_ids - group * BUS_DEV
    grp[...] = group.astype(F32)
    hi[...] = (offset >> 8).astype(F32)
    lo[...] = (offset & 255).astype(F32)

    sub16 = iota((16, 128), 0)

    def lanes(c, width=128):
        return pl.ds(pl.multiple_of(c * width, width), width)

    def mark(c, _):
        row = grp[pl.ds(c, 1), :]
        g01[pl.ds(pl.multiple_of(c * 16, 16), 16), :] = jnp.where(row == sub16, 1.0, 0.0).astype(BF16)
        digits = jnp.where(sub16 == 0, hi[pl.ds(c, 1), :], jnp.where(sub16 == 1, lo[pl.ds(c, 1), :], 0.0))
        xa[pl.ds(DIGITS, 16), lanes(c)] = digits.astype(BF16)
        return 0

    lax.fori_loop(0, CHUNKS, mark, 0)
    ahead = lax.broadcasted_iota(jnp.int32, (128, 256), 0)
    place = lax.broadcasted_iota(jnp.int32, (128, 256), 1)
    steps = jnp.where((ahead <= place) | (place >= 128), 1.0, 0.0).astype(BF16)
    pre[...] = jnp.dot(g01[...], steps, preferred_element_type=F32)
    sub256 = iota((256, 128), 0)

    def rank(c, run):
        rows = pl.ds(pl.multiple_of(c * 16, 16), 16)
        counted = g01[rows, :].astype(F32) * (pre[rows, pl.ds(0, 128)] + run)
        position = jnp.sum(counted, axis=0, keepdims=True) - 1.0
        bt[:, lanes(c)] = jnp.where(position == sub256, 1.0, 0.0).astype(BF16)
        return run + pre[rows, pl.ds(128, 128)]

    lax.fori_loop(0, CHUNKS, rank, jnp.zeros((16, 128), F32))
    for copy in val_copies:
        copy.wait()

    def narrow(c, _):
        xa[pl.ds(0, 32), lanes(c)] = raw[pl.ds(0, 32), lanes(c)].astype(BF16)
        xa[pl.ds(48, 32), lanes(c)] = raw[pl.ds(48, 32), lanes(c)].astype(BF16)
        return 0

    lax.fori_loop(0, CHUNKS, narrow, 0)

    sv, rv = (sv0, sv1), (rv0, rv1)

    def chosen(row, value, vals):
        mask = jnp.where(jnp.broadcast_to(row, (16, row.shape[1])) == value, 1.0, 0.0).astype(BF16)
        return vals * jnp.concatenate([mask] * (vals.shape[0] // 16), axis=0)

    def pack(half):
        rows = ROWS[half]
        first = half * ROWS[0]
        for batch in range(2):
            owners = [(bus + batch * 8 + i + 1) % BUSES for i in range(8)]
            owners_f = [o.astype(F32) for o in owners]

            def pick(c, _):
                row = grp[pl.ds(c, 1), :]
                vals = xa[pl.ds(first, rows), lanes(c)]
                for i in range(8):
                    lhs[pl.ds(i * rows, rows), lanes(c)] = chosen(row, owners_f[i], vals)
                return 0

            lax.fori_loop(0, CHUNKS, pick, 0)
            packed = lax.dot_general(
                lhs[pl.ds(0, 8 * rows), :], bt[...], NT, preferred_element_type=F32
            ).astype(BF16)
            for i in range(8):
                j = batch * 8 + i
                if j < BUSES - 1:
                    sv[half][j] = packed[i * rows:(i + 1) * rows]
                    pltpu.make_async_remote_copy(
                        sv[half].at[j], rv[half].at[bus], xs_sem.at[half, j], xr_sem.at[half, bus],
                        device_id=(line, owners[i]), device_id_type=MESH,
                    ).start()
                else:
                    rv[half][bus] = packed[i * rows:(i + 1) * rows]

    def received(half):
        for j in range(1, BUSES):
            src = (bus + j) % BUSES
            pltpu.make_async_copy(rv[half].at[src], rv[half].at[src], xr_sem.at[half, src]).wait()

    def low_digit(k, _):
        row = rv0[k, pl.ds(DIGITS, 16), :].astype(F32)[1:2]
        bt[:, lanes(k, 256)] = jnp.where(row == iota((256, 256), 0), 1.0, 0.0).astype(BF16)
        return 0

    def spread(half, inj):
        for part in range(2):

            def high_digit(k, _):
                vals = rv[half][k, pl.ds(0, 32), :]
                row = rv0[k, pl.ds(DIGITS, 16), :].astype(F32)[0:1]
                for i in range(9):
                    lhs[pl.ds(i * 32, 32), lanes(k, 256)] = chosen(row, float(part * 9 + i), vals)
                return 0

            lax.fori_loop(0, BUSES, high_digit, 0)
            sums = lax.dot_general(
                lhs[pl.ds(0, 288), :], bt[...], NT, preferred_element_type=F32
            ).astype(BF16)
            for i in range(9):
                for t in range(2):
                    strip = 2 * (part * 9 + i) + t
                    if strip < ZONES * 5:
                        zone, lane = strip // 5, (strip % 5) * 128
                        inj[zone, pl.ds(pl.multiple_of(line * 32, 32), 32), lane:lane + 128] = sums[
                            i * 32:(i + 1) * 32, t * 128:t * 128 + 128
                        ]

    def gather(half, number, owner, first, count, target):
        buf = inj1 if half else inj0
        rows = buf.at[pl.ds(0, ZONES), pl.ds(pl.multiple_of(owner * 32, 32) + first, count)]
        return pltpu.make_async_remote_copy(
            rows, rows, gs_sem.at[half, number], gr_sem.at[half, number],
            device_id=(target, bus), device_id_type=MESH,
        )

    def arrival(half, number, owner, first, count):
        buf = inj1 if half else inj0
        rows = buf.at[pl.ds(0, ZONES), pl.ds(pl.multiple_of(owner * 32, 32) + first, count)]
        return pltpu.make_async_copy(rows, rows, gr_sem.at[half, number])

    far = ((y + 2) % RING) * 2 + core
    sib_up = ((y + 1) % RING) * 2 + (1 - core)
    sib_down = ((y + 3) % RING) * 2 + (1 - core)
    sib_far = ((y + 2) % RING) * 2 + (1 - core)

    ROUTES = (
        (line, 0, 32, up),
        (line, 0, 32, down),
        (line, 0, 32, sib),
        (down, 0, 16, up),
        (down, 0, 32, sib),
        (up, 16, 16, down),
        (up, 0, 32, sib),
        (far, 0, 16, sib),
        (far, 16, 16, sib),
    )

    def route(half, number):
        return gather(half, number, *ROUTES[number])

    def gather_start(half):
        for number in range(3):
            route(half, number).start()

    def gather_relay(half):
        arrival(half, 0, down, 0, 32).wait()
        route(half, 3).start()
        route(half, 4).start()
        arrival(half, 1, up, 0, 32).wait()
        route(half, 5).start()
        route(half, 6).start()

    def gather_last(half):
        arrival(half, 3, far, 0, 16).wait()
        route(half, 7).start()
        arrival(half, 5, far, 16, 16).wait()
        route(half, 8).start()

    def gather_finish(half):
        arrival(half, 2, sib, 0, 32).wait()
        arrival(half, 4, sib_down, 0, 32).wait()
        arrival(half, 6, sib_up, 0, 32).wait()
        arrival(half, 7, sib_far, 0, 16).wait()
        arrival(half, 8, sib_far, 16, 16).wait()

    pl.semaphore_wait(barrier, BUSES - 1 + 3)
    pack(0)
    pack(1)
    received(0)
    lax.fori_loop(0, BUSES, low_digit, 0)
    spread(0, inj0)
    gather_start(0)
    received(1)
    spread(1, inj1)
    gather_relay(0)
    gather_start(1)
    gather_last(0)
    gather_finish(0)
    for copy in small_copies:
        copy.wait()

    A, B = pl.ds(0, 256), pl.ds(256, 256)
    L, R = pl.ds(0, 128), pl.ds(128, 128)
    LO, HI = pl.ds(0, 2), pl.ds(2, 2)
    ALL = pl.ds(0, 4)

    def push(src, dst, t, step, device):
        pltpu.make_async_remote_copy(
            src, dst, fs_sem.at[t, step], fr_sem.at[t, step],
            device_id=(line, device), device_id_type=MESH,
        ).start()

    xp, xm, zp, zm = x1 * RING + z, x3 * RING + z, x * RING + z1, x * RING + z3

    def produce(t, zone, inj):
        for slot in range(SLOTS):
            @pl.when(t < LZ)
            def _():
                block_copy(zone, slot).wait()
        live = live_ref[0, zone]
        pieces = []
        for slot in range(SLOTS):
            at = jnp.where(slot < live, slot_ref[slot, zone], ZONES)
            pieces.append(inj[at])
        out = lax.dot_general(
            jnp.concatenate(pieces, axis=1), blk[zone], NT, preferred_element_type=F32
        ).astype(BF16)
        flows[t] = out.reshape(RING, RING, 16, ZL)
        push(flows.at[t, x2, LO, :, A], ra.at[t, 0], t, 0, xp)
        push(flows.at[t, x2, HI, :, A], ra.at[t, 1], t, 0, xm)
        push(flows.at[t, LO, z2, :, B], ra.at[t, 2], t, 0, zp)
        push(flows.at[t, HI, z2, :, B], ra.at[t, 3], t, 0, zm)

    def arrived(buf, t, step):
        pltpu.make_async_copy(buf.at[t], buf.at[t], fr_sem.at[t, step]).wait()

    def add(a, b):
        return (a.astype(F32) + b.astype(F32)).astype(BF16)

    def first_b(t):
        arrived(ra, t, 0)
        flows[t, x1, LO, :, A] = add(flows[t, x1, LO, :, A], ra[t, 0])
        push(flows.at[t, x1, ALL, :, A], rb.at[t, 0], t, 1, xp)
        flows[t, x3, HI, :, A] = add(flows[t, x3, HI, :, A], ra[t, 1])
        push(flows.at[t, x3, ALL, :, A], rb.at[t, 1], t, 1, xm)
        flows[t, LO, z1, :, B] = add(flows[t, LO, z1, :, B], ra[t, 2])
        push(flows.at[t, ALL, z1, :, B], rb.at[t, 2], t, 1, zp)
        flows[t, HI, z3, :, B] = add(flows[t, HI, z3, :, B], ra[t, 3])
        push(flows.at[t, ALL, z3, :, B], rb.at[t, 3], t, 1, zm)

    def add3(a, b, c):
        return a.astype(F32) + b.astype(F32) + c.astype(F32)

    def second_a(t):
        arrived(rb, t, 1)
        sa[t, 0] = add3(flows[t, x, ALL, :, A], rb[t, 0], rb[t, 1]).astype(BF16)
        push(sa.at[t, 0, z2, :, L], rc.at[t, 0], t, 2, zp)
        push(sa.at[t, 0, z2, :, R], rc.at[t, 1], t, 2, zm)
        sa[t, 1] = add3(flows[t, ALL, z, :, B], rb[t, 2], rb[t, 3]).astype(BF16)
        push(sa.at[t, 1, x2, :, L], rc.at[t, 2], t, 2, xp)
        push(sa.at[t, 1, x2, :, R], rc.at[t, 3], t, 2, xm)

    def second_b(t):
        arrived(rc, t, 2)
        sa[t, 0, z1, :, L] = add(sa[t, 0, z1, :, L], rc[t, 0])
        push(sa.at[t, 0, z1], rd.at[t, 0], t, 3, zp)
        sa[t, 0, z3, :, R] = add(sa[t, 0, z3, :, R], rc[t, 1])
        push(sa.at[t, 0, z3], rd.at[t, 1], t, 3, zm)
        sa[t, 1, x1, :, L] = add(sa[t, 1, x1, :, L], rc[t, 2])
        push(sa.at[t, 1, x1], rd.at[t, 2], t, 3, xp)
        sa[t, 1, x3, :, R] = add(sa[t, 1, x3, :, R], rc[t, 3])
        push(sa.at[t, 1, x3], rd.at[t, 3], t, 3, xm)

    def finish(t, zone, half):
        arrived(rd, t, 3)
        ratings = jnp.concatenate([rating_ref[pl.ds(zone * 4 + i, 1), :] for i in range(4)], axis=1)
        flow = jnp.concatenate(
            [add3(sa[t, 0, z], rd[t, 0], rd[t, 1]), add3(sa[t, 1, x], rd[t, 2], rd[t, 3])], axis=1
        )
        loading = flow / ratings
        load_ref[pl.ds(pl.multiple_of(half * 16, 16), 16), lanes(zone, ZL)] = loading
        top = jnp.max(jnp.abs(loading), axis=0, keepdims=True)
        for i in range(4):
            row = pl.ds(zone * 4 + i, 1)
            wl[row, :] = jnp.maximum(wl[row, :], top[:, i * 128:(i + 1) * 128])
        for step, buf in enumerate((ra, rb, rc, rd)):
            pltpu.make_async_copy(buf.at[t], buf.at[t], fs_sem.at[t, step]).wait()

    parts = (pl.ds(0, WSPLIT * 4), pl.ds(WSPLIT * 4, 48 - WSPLIT * 4))

    def share(part):
        for j in range(1, BUSES):
            pltpu.make_async_remote_copy(
                wl.at[parts[part]], wr.at[bus, parts[part]], ws_sem.at[part, j], wr_sem.at[part, bus],
                device_id=(line, (bus + j) % BUSES), device_id_type=MESH,
            ).start()

    def stages(t):
        d1, d2, d3, d4 = LAG

        def when(lag, stage):
            @pl.when((t >= lag) & (t < T + lag))
            def _():
                stage(t - lag)

        when(d1, first_b)
        when(d2, second_a)
        when(d3, second_b)

        @pl.when((t >= d4) & (t < T + d4))
        def _():
            finish(t - d4, (t - d4) % LZ, (t - d4) // LZ)

        @pl.when(t == d4 + LZ + WSPLIT - 1)
        def _():
            share(0)

    def first_half(t, _):
        produce(t, t, inj0)

        @pl.when(t == 4)
        def _():
            gather_relay(1)

        @pl.when(t == 8)
        def _():
            gather_last(1)

        stages(t)
        return 0

    def second_half(t, _):
        produce(t, t - LZ, inj1)
        stages(t)
        return 0

    def drain(t, _):
        stages(t)
        return 0

    lax.fori_loop(0, LZ, first_half, 0)
    gather_finish(1)
    lax.fori_loop(LZ, T, second_half, 0)
    lax.fori_loop(T, T + LAG[3], drain, 0)

    share(1)
    for half in range(2):
        for number in range(len(ROUTES)):
            route(half, number).wait_send()
        for j in range(BUSES - 1):
            pltpu.make_async_copy(sv[half].at[j], sv[half].at[j], xs_sem.at[half, j]).wait()
    best = wl[...]
    for part in range(2):
        for j in range(1, BUSES):
            src = wr.at[(bus + j) % BUSES, parts[part]]
            pltpu.make_async_copy(src, src, wr_sem.at[part, (bus + j) % BUSES]).wait()
    for j in range(1, BUSES):
        best = jnp.maximum(best, wr[(bus + j) % BUSES])
    worst_ref[...] = best[0:LZ * 4]
    for part in range(2):
        for j in range(1, BUSES):
            src = wl.at[parts[part]]
            pltpu.make_async_copy(src, src, ws_sem.at[part, j]).wait()


def hand_over(load_in, worst_in, load_ref, worst_ref):
    load_ref[...] = load_in[...]
    worst_ref[...] = worst_in[...]


def body(site_values, site_bus, block_count, block_zone, ptdf_blocks, rating):
    hbm = pl.BlockSpec(memory_space=pl.ANY)
    vmem = pl.BlockSpec(memory_space=pltpu.VMEM)
    dma = pltpu.SemaphoreType.DMA
    loading, worst = pl.pallas_call(
        kernel,
        out_shape=(
            jax.ShapeDtypeStruct((32, LZ * ZL), F32),
            jax.ShapeDtypeStruct((LZ * 4, 128), F32),
        ),
        in_specs=[hbm, hbm, hbm, hbm, hbm, vmem],
        out_specs=(vmem, vmem),
        scratch_shapes=[
            pltpu.SMEM((1, LZ), jnp.int32),
            pltpu.SMEM((SLOTS, LZ), jnp.int32),
            pltpu.VMEM((CHUNKS, 128), jnp.int32),
            pltpu.VMEM((CHUNKS, 128), F32),
            pltpu.VMEM((CHUNKS, 128), F32),
            pltpu.VMEM((CHUNKS, 128), F32),
            pltpu.VMEM((ROWS_ALL, SITE_DEV), F32),
            pltpu.VMEM((ROWS_ALL, SITE_DEV), BF16),
            pltpu.VMEM((CHUNKS * 16, 128), BF16),
            pltpu.VMEM((CHUNKS * 16, 256), F32),
            pltpu.VMEM((256, SITE_DEV), BF16),
            pltpu.VMEM((384, SITE_DEV), BF16),
            pltpu.VMEM((BUSES - 1, ROWS[0], PER), BF16),
            pltpu.VMEM((BUSES - 1, ROWS[1], PER), BF16),
            pltpu.VMEM((BUSES, ROWS[0], PER), BF16),
            pltpu.VMEM((BUSES, ROWS[1], PER), BF16),
            pltpu.VMEM((LZ, ZL, SLOTS * ZB), BF16),
            pltpu.VMEM((ZONES + 1, HALF, ZB), BF16),
            pltpu.VMEM((ZONES + 1, HALF, ZB), BF16),
            pltpu.VMEM((T, RING, RING, 16, ZL), BF16),
            pltpu.VMEM((T, 4, 2, 16, 256), BF16),
            pltpu.VMEM((T, 4, 4, 16, 256), BF16),
            pltpu.VMEM((T, 2, 4, 16, 256), BF16),
            pltpu.VMEM((T, 4, 16, 128), BF16),
            pltpu.VMEM((T, 4, 16, 256), BF16),
            pltpu.VMEM((48, 128), F32),
            pltpu.VMEM((BUSES, 48, 128), F32),
            dma((7,)),
            dma((LZ, SLOTS)),
            dma((2, BUSES)),
            dma((2, BUSES)),
            dma((2, 9)),
            dma((2, 9)),
            dma((T, 4)),
            dma((T, 4)),
            dma((2, BUSES)),
            dma((2, BUSES)),
        ],
        compiler_params=pltpu.CompilerParams(
            collective_id=0, has_side_effects=True, vmem_limit_bytes=62 * 1024 * 1024
        ),
        name="screen",
    )(
        block_count.T, block_zone.T, site_values, site_bus.reshape(-1, 128), ptdf_blocks,
        rating.reshape(-1, 128),
    )
    loading, worst = pl.pallas_call(
        hand_over,
        out_shape=(
            jax.ShapeDtypeStruct((32, LZ * ZL), F32),
            jax.ShapeDtypeStruct((LZ * 4, 128), F32),
        ),
        in_specs=[vmem, vmem],
        out_specs=(vmem, vmem),
        name="hand_over",
    )(loading, worst)
    return loading, worst.reshape(-1)


def solution(mesh):
    return jax.shard_map(
        body,
        mesh=mesh,
        in_specs=(
            P("line", "bus"),
            P(),
            P("line", "bus"),
            P("line", "bus"),
            P("line", "bus", None, None),
            P("line"),
        ),
        out_specs=(P("bus", "line"), P("line")),
        check_vma=False,
    )
```

```python
import functools

import jax
import jax.numpy as jnp
from jax import lax
from jax.experimental import pallas as pl
from jax.experimental.pallas import tpu as pltpu
from jax.sharding import PartitionSpec as P

MESH = pl.DeviceIdType.MESH
F32 = jnp.float32
BF16 = jnp.bfloat16

LINES = 8
BUSES = 16
RING = 4
BUS_DEV = 4480
SCEN_DEV = 64
SITE_DEV = 4096
PER = 256
ROWS = (48, 32)
ROWS_ALL = 80
DIGITS = 32
CHUNKS = SITE_DEV // 128
ZONES = 7
ZB = 640
LZ = 11
ZL = 512
SLOTS = 3
HALF = 256
T = 2 * LZ
NT = (((1,), (1,)), ((), ()))
LAG = (4, 8, 12, 16)
GATHERS = ((0, 0, 3), (0, 3, 4), (1, 0, 7))
SHARES = (4, 8, 10, 12)


def iota(shape, dim):
    return lax.broadcasted_iota(jnp.int32, shape, dim).astype(F32)


def kernel(
    count_hbm, zone_hbm, values_hbm, bus_hbm, blocks_hbm, rating_ref,
    load_ref, worst_ref,
    live_ref, slot_ref, ids, grp, hi, lo, raw, xa, g01, pre, bt, lhs, sv0, sv1, rv0, rv1, blk, inj0, inj1,
    flows, ra, rb, sa, rc, rd, wl, wr,
    in_sem, blk_sem, xs_sem, xr_sem, gs_sem, gr_sem, fs_sem, fr_sem, ws_sem, wr_sem,
):
    line = lax.axis_index("line")
    bus = lax.axis_index("bus")
    y, core = line // 2, line % 2
    x, z = bus // RING, bus % RING
    up = ((y + 1) % RING) * 2 + core
    down = ((y + 3) % RING) * 2 + core
    sib = y * 2 + (1 - core)
    x1, x2, x3 = (x + 1) % RING, (x + 2) % RING, (x + 3) % RING
    z1, z2, z3 = (z + 1) % RING, (z + 2) % RING, (z + 3) % RING

    barrier = pltpu.get_barrier_semaphore()
    for j in range(1, BUSES):
        pl.semaphore_signal(barrier, inc=1, device_id=(line, (bus + j) % BUSES), device_id_type=MESH)
    for other in (up, down, sib):
        pl.semaphore_signal(barrier, inc=1, device_id=(other, bus), device_id_type=MESH)

    ids_copy = pltpu.make_async_copy(bus_hbm.at[pl.ds(bus * CHUNKS, CHUNKS)], ids, in_sem.at[0])
    ids_copy.start()
    val_copies = [
        pltpu.make_async_copy(values_hbm.at[pl.ds(16 * q, 16)], raw.at[pl.ds(row, 16)], in_sem.at[1 + q])
        for q, row in enumerate((0, 48, 16, 64))
    ]
    for copy in val_copies:
        copy.start()
    small_copies = [
        pltpu.make_async_copy(count_hbm, live_ref, in_sem.at[5]),
        pltpu.make_async_copy(zone_hbm, slot_ref, in_sem.at[6]),
    ]
    for copy in small_copies:
        copy.start()

    def block_copy(zone, slot):
        return pltpu.make_async_copy(
            blocks_hbm.at[zone, slot], blk.at[zone, :, pl.ds(slot * ZB, ZB)], blk_sem.at[zone, slot]
        )

    def start_blocks(zone, _):
        for slot in range(SLOTS):
            block_copy(zone, slot).start()
        return 0

    lax.fori_loop(0, LZ, start_blocks, 0)

    inj0[ZONES] = jnp.zeros((HALF, ZB), BF16)
    inj1[ZONES] = jnp.zeros((HALF, ZB), BF16)
    wl[...] = jnp.zeros_like(wl)
    ids_copy.wait()
    bus_ids = ids[...]
    group = jnp.zeros_like(bus_ids)
    for g in range(1, BUSES):
        group = group + (bus_ids >= g * BUS_DEV).astype(jnp.int32)
    offset = bus_ids - group * BUS_DEV
    grp[...] = group.astype(F32)
    hi[...] = (offset >> 8).astype(F32)
    lo[...] = (offset & 255).astype(F32)

    sub16 = iota((16, 128), 0)

    def lanes(c, width=128):
        return pl.ds(pl.multiple_of(c * width, width), width)

    def mark(c, _):
        row = grp[pl.ds(c, 1), :]
        g01[pl.ds(pl.multiple_of(c * 16, 16), 16), :] = jnp.where(row == sub16, 1.0, 0.0).astype(BF16)
        digits = jnp.where(sub16 == 0, hi[pl.ds(c, 1), :], jnp.where(sub16 == 1, lo[pl.ds(c, 1), :], 0.0))
        xa[pl.ds(DIGITS, 16), lanes(c)] = digits.astype(BF16)
        return 0

    lax.fori_loop(0, CHUNKS, mark, 0)
    ahead = lax.broadcasted_iota(jnp.int32, (128, 256), 0)
    place = lax.broadcasted_iota(jnp.int32, (128, 256), 1)
    steps = jnp.where((ahead <= place) | (place >= 128), 1.0, 0.0).astype(BF16)
    pre[...] = jnp.dot(g01[...], steps, preferred_element_type=F32)
    sub256 = iota((256, 128), 0)

    def rank(c, run):
        rows = pl.ds(pl.multiple_of(c * 16, 16), 16)
        counted = g01[rows, :].astype(F32) * (pre[rows, pl.ds(0, 128)] + run)
        position = jnp.sum(counted, axis=0, keepdims=True) - 1.0
        bt[:, lanes(c)] = jnp.where(position == sub256, 1.0, 0.0).astype(BF16)
        return run + pre[rows, pl.ds(128, 128)]

    lax.fori_loop(0, CHUNKS, rank, jnp.zeros((16, 128), F32))
    for copy in val_copies:
        copy.wait()

    def narrow(c, _):
        xa[pl.ds(0, 32), lanes(c)] = raw[pl.ds(0, 32), lanes(c)].astype(BF16)
        xa[pl.ds(48, 32), lanes(c)] = raw[pl.ds(48, 32), lanes(c)].astype(BF16)
        return 0

    lax.fori_loop(0, CHUNKS, narrow, 0)

    sv, rv = (sv0, sv1), (rv0, rv1)

    def chosen(row, value, vals):
        mask = jnp.where(jnp.broadcast_to(row, (16, row.shape[1])) == value, 1.0, 0.0).astype(BF16)
        return vals * jnp.concatenate([mask] * (vals.shape[0] // 16), axis=0)

    def pack(half):
        rows = ROWS[half]
        first = half * ROWS[0]
        for batch in range(2):
            owners = [(bus + batch * 8 + i + 1) % BUSES for i in range(8)]
            owners_f = [o.astype(F32) for o in owners]

            def pick(c, _):
                row = grp[pl.ds(c, 1), :]
                vals = xa[pl.ds(first, rows), lanes(c)]
                for i in range(8):
                    lhs[pl.ds(i * rows, rows), lanes(c)] = chosen(row, owners_f[i], vals)
                return 0

            lax.fori_loop(0, CHUNKS, pick, 0)
            packed = lax.dot_general(
                lhs[pl.ds(0, 8 * rows), :], bt[...], NT, preferred_element_type=F32
            ).astype(BF16)
            if half == 0 and batch == 0:
                pl.semaphore_wait(barrier, BUSES - 1 + 3)
            for i in range(8):
                j = batch * 8 + i
                if j < BUSES - 1:
                    sv[half][j] = packed[i * rows:(i + 1) * rows]
                    pltpu.make_async_remote_copy(
                        sv[half].at[j], rv[half].at[bus], xs_sem.at[half, j], xr_sem.at[half, bus],
                        device_id=(line, owners[i]), device_id_type=MESH,
                    ).start()
                else:
                    rv[half][bus] = packed[i * rows:(i + 1) * rows]

    def received(half):
        for j in range(1, BUSES):
            src = (bus + j) % BUSES
            pltpu.make_async_copy(rv[half].at[src], rv[half].at[src], xr_sem.at[half, src]).wait()

    def low_digit(k, _):
        row = rv0[k, pl.ds(DIGITS, 16), :].astype(F32)[1:2]
        bt[:, lanes(k, 256)] = jnp.where(row == iota((256, 256), 0), 1.0, 0.0).astype(BF16)
        return 0

    def spread(half, inj, after):
        for part in range(2):

            def high_digit(k, _):
                vals = rv[half][k, pl.ds(0, 32), :]
                row = rv0[k, pl.ds(DIGITS, 16), :].astype(F32)[0:1]
                for i in range(9):
                    lhs[pl.ds(i * 32, 32), lanes(k, 256)] = chosen(row, float(part * 9 + i), vals)
                return 0

            lax.fori_loop(0, BUSES, high_digit, 0)
            sums = lax.dot_general(
                lhs[pl.ds(0, 288), :], bt[...], NT, preferred_element_type=F32
            ).astype(BF16)
            for i in range(9):
                for t in range(2):
                    strip = 2 * (part * 9 + i) + t
                    if strip < ZONES * 5:
                        zone, lane = strip // 5, (strip % 5) * 128
                        inj[zone, pl.ds(pl.multiple_of(line * 32, 32), 32), lane:lane + 128] = sums[
                            i * 32:(i + 1) * 32, t * 128:t * 128 + 128
                        ]
            after[part]()

    def gathered(step, owner, first, count):
        half, zone, zones = GATHERS[step]
        rows = pl.ds(pl.multiple_of(owner * 32, 32) + first, count)
        return (inj1 if half else inj0).at[pl.ds(zone, zones), rows]

    def gather(step, number, owner, first, count, target):
        rows = gathered(step, owner, first, count)
        return pltpu.make_async_remote_copy(
            rows, rows, gs_sem.at[step, number], gr_sem.at[step, number],
            device_id=(target, bus), device_id_type=MESH,
        )

    def arrival(step, number, owner, first, count):
        rows = gathered(step, owner, first, count)
        return pltpu.make_async_copy(rows, rows, gr_sem.at[step, number])

    far = ((y + 2) % RING) * 2 + core
    sib_up = ((y + 1) % RING) * 2 + (1 - core)
    sib_down = ((y + 3) % RING) * 2 + (1 - core)
    sib_far = ((y + 2) % RING) * 2 + (1 - core)

    ROUTES = (
        (line, 0, 32, up),
        (line, 0, 32, down),
        (line, 0, 32, sib),
        (down, 0, 16, up),
        (down, 0, 32, sib),
        (up, 16, 16, down),
        (up, 0, 32, sib),
        (far, 0, 16, sib),
        (far, 16, 16, sib),
    )

    def route(step, number):
        return gather(step, number, *ROUTES[number])

    def gather_start(step):
        for number in range(3):
            route(step, number).start()

    def gather_relay(step):
        arrival(step, 0, down, 0, 32).wait()
        route(step, 3).start()
        route(step, 4).start()
        arrival(step, 1, up, 0, 32).wait()
        route(step, 5).start()
        route(step, 6).start()

    def gather_last(step):
        arrival(step, 3, far, 0, 16).wait()
        route(step, 7).start()
        arrival(step, 5, far, 16, 16).wait()
        route(step, 8).start()

    def gather_finish(step):
        arrival(step, 2, sib, 0, 32).wait()
        arrival(step, 4, sib_down, 0, 32).wait()
        arrival(step, 6, sib_up, 0, 32).wait()
        arrival(step, 7, sib_far, 0, 16).wait()
        arrival(step, 8, sib_far, 16, 16).wait()

    pack(0)
    pack(1)
    received(0)
    lax.fori_loop(0, BUSES, low_digit, 0)
    spread(0, inj0, (lambda: gather_start(0), lambda: gather_start(1)))
    received(1)
    spread(1, inj1, (lambda: gather_relay(0), lambda: gather_relay(1)))
    gather_start(2)
    for step in range(2):
        gather_last(step)
    for step in range(2):
        gather_finish(step)
    for copy in small_copies:
        copy.wait()

    A, B = pl.ds(0, 256), pl.ds(256, 256)
    L, R = pl.ds(0, 128), pl.ds(128, 128)
    LO, HI = pl.ds(0, 2), pl.ds(2, 2)
    ALL = pl.ds(0, 4)

    def push(src, dst, t, step, device):
        pltpu.make_async_remote_copy(
            src, dst, fs_sem.at[t, step], fr_sem.at[t, step],
            device_id=(line, device), device_id_type=MESH,
        ).start()

    xp, xm, zp, zm = x1 * RING + z, x3 * RING + z, x * RING + z1, x * RING + z3

    def produce(t, zone, inj):
        for slot in range(SLOTS):
            @pl.when(t < LZ)
            def _():
                block_copy(zone, slot).wait()
        live = live_ref[0, zone]
        pieces = []
        for slot in range(SLOTS):
            at = jnp.where(slot < live, slot_ref[slot, zone], ZONES)
            pieces.append(inj[at])
        out = lax.dot_general(
            jnp.concatenate(pieces, axis=1), blk[zone], NT, preferred_element_type=F32
        ).astype(BF16)
        flows[t] = out.reshape(RING, RING, 16, ZL)
        push(flows.at[t, x2, LO, :, A], ra.at[t, 0], t, 0, xp)
        push(flows.at[t, x2, HI, :, A], ra.at[t, 1], t, 0, xm)
        push(flows.at[t, LO, z2, :, B], ra.at[t, 2], t, 0, zp)
        push(flows.at[t, HI, z2, :, B], ra.at[t, 3], t, 0, zm)

    def arrived(buf, t, step):
        pltpu.make_async_copy(buf.at[t], buf.at[t], fr_sem.at[t, step]).wait()

    def add(a, b):
        return (a.astype(F32) + b.astype(F32)).astype(BF16)

    def first_b(t):
        arrived(ra, t, 0)
        sums = (
            add(flows[t, x1, LO, :, A], ra[t, 0]),
            add(flows[t, x3, HI, :, A], ra[t, 1]),
            add(flows[t, LO, z1, :, B], ra[t, 2]),
            add(flows[t, HI, z3, :, B], ra[t, 3]),
        )
        flows[t, x1, LO, :, A] = sums[0]
        flows[t, x3, HI, :, A] = sums[1]
        flows[t, LO, z1, :, B] = sums[2]
        flows[t, HI, z3, :, B] = sums[3]
        push(flows.at[t, x1, ALL, :, A], rb.at[t, 0], t, 1, xp)
        push(flows.at[t, x3, ALL, :, A], rb.at[t, 1], t, 1, xm)
        push(flows.at[t, ALL, z1, :, B], rb.at[t, 2], t, 1, zp)
        push(flows.at[t, ALL, z3, :, B], rb.at[t, 3], t, 1, zm)

    def add3(a, b, c):
        return a.astype(F32) + b.astype(F32) + c.astype(F32)

    def second_a(t):
        arrived(rb, t, 1)
        sums = (
            add3(flows[t, x, ALL, :, A], rb[t, 0], rb[t, 1]).astype(BF16),
            add3(flows[t, ALL, z, :, B], rb[t, 2], rb[t, 3]).astype(BF16),
        )
        sa[t, 0] = sums[0]
        sa[t, 1] = sums[1]
        push(sa.at[t, 0, z2, :, L], rc.at[t, 0], t, 2, zp)
        push(sa.at[t, 0, z2, :, R], rc.at[t, 1], t, 2, zm)
        push(sa.at[t, 1, x2, :, L], rc.at[t, 2], t, 2, xp)
        push(sa.at[t, 1, x2, :, R], rc.at[t, 3], t, 2, xm)

    def second_b(t):
        arrived(rc, t, 2)
        sums = (
            add(sa[t, 0, z1, :, L], rc[t, 0]),
            add(sa[t, 0, z3, :, R], rc[t, 1]),
            add(sa[t, 1, x1, :, L], rc[t, 2]),
            add(sa[t, 1, x3, :, R], rc[t, 3]),
        )
        sa[t, 0, z1, :, L] = sums[0]
        sa[t, 0, z3, :, R] = sums[1]
        sa[t, 1, x1, :, L] = sums[2]
        sa[t, 1, x3, :, R] = sums[3]
        push(sa.at[t, 0, z1], rd.at[t, 0], t, 3, zp)
        push(sa.at[t, 0, z3], rd.at[t, 1], t, 3, zm)
        push(sa.at[t, 1, x1], rd.at[t, 2], t, 3, xp)
        push(sa.at[t, 1, x3], rd.at[t, 3], t, 3, xm)

    def finish(t, zone, half):
        arrived(rd, t, 3)
        ratings = jnp.concatenate([rating_ref[pl.ds(zone * 4 + i, 1), :] for i in range(4)], axis=1)
        flow = jnp.concatenate(
            [add3(sa[t, 0, z], rd[t, 0], rd[t, 1]), add3(sa[t, 1, x], rd[t, 2], rd[t, 3])], axis=1
        )
        loading = flow / ratings
        load_ref[pl.ds(pl.multiple_of(half * 16, 16), 16), lanes(zone, ZL)] = loading
        top = jnp.max(jnp.abs(loading), axis=0, keepdims=True)
        for i in range(4):
            row = pl.ds(zone * 4 + i, 1)
            wl[row, :] = jnp.maximum(wl[row, :], top[:, i * 128:(i + 1) * 128])
        for step, buf in enumerate((ra, rb, rc, rd)):
            pltpu.make_async_copy(buf.at[t], buf.at[t], fs_sem.at[t, step]).wait()

    parts = [pl.ds(first * 4, (last - first) * 4) for first, last in zip((0, *SHARES), SHARES)]

    def share(part):
        for j in range(1, BUSES):
            pltpu.make_async_remote_copy(
                wl.at[parts[part]], wr.at[bus, parts[part]], ws_sem.at[part, j], wr_sem.at[part, bus],
                device_id=(line, (bus + j) % BUSES), device_id_type=MESH,
            ).start()

    def stages(t):
        d1, d2, d3, d4 = LAG

        def when(lag, stage):
            @pl.when((t >= lag) & (t < T + lag))
            def _():
                stage(t - lag)

        when(d1, first_b)
        when(d2, second_a)
        when(d3, second_b)

        @pl.when((t >= d4) & (t < T + d4))
        def _():
            finish(t - d4, (t - d4) % LZ, (t - d4) // LZ)

        for part in range(len(parts) - 1):
            @pl.when(t == d4 + LZ + SHARES[part] - 1)
            def _(part=part):
                share(part)

    def first_half(t, _):
        produce(t, t, inj0)

        @pl.when(t == 4)
        def _():
            gather_relay(2)

        @pl.when(t == 8)
        def _():
            gather_last(2)

        stages(t)
        return 0

    def second_half(t, _):
        produce(t, t - LZ, inj1)
        stages(t)
        return 0

    def drain(t, _):
        stages(t)
        return 0

    lax.fori_loop(0, LZ, first_half, 0)
    gather_finish(2)
    lax.fori_loop(LZ, T, second_half, 0)
    lax.fori_loop(T, T + LAG[3], drain, 0)

    share(len(parts) - 1)
    for step in range(len(GATHERS)):
        for number in range(len(ROUTES)):
            route(step, number).wait_send()
    for half in range(2):
        for j in range(BUSES - 1):
            pltpu.make_async_copy(sv[half].at[j], sv[half].at[j], xs_sem.at[half, j]).wait()
    best = wl[...]
    for part in range(len(parts)):
        for j in range(1, BUSES):
            src = wr.at[(bus + j) % BUSES, parts[part]]
            pltpu.make_async_copy(src, src, wr_sem.at[part, (bus + j) % BUSES]).wait()
    for j in range(1, BUSES):
        best = jnp.maximum(best, wr[(bus + j) % BUSES])
    worst_ref[...] = best[0:LZ * 4]
    for part in range(len(parts)):
        for j in range(1, BUSES):
            src = wl.at[parts[part]]
            pltpu.make_async_copy(src, src, ws_sem.at[part, j]).wait()


def hand_over(load_in, worst_in, load_ref, worst_ref):
    load_ref[...] = load_in[...]
    worst_ref[...] = worst_in[...]


def body(site_values, site_bus, block_count, block_zone, ptdf_blocks, rating):
    hbm = pl.BlockSpec(memory_space=pl.ANY)
    vmem = pl.BlockSpec(memory_space=pltpu.VMEM)
    dma = pltpu.SemaphoreType.DMA
    loading, worst = pl.pallas_call(
        kernel,
        out_shape=(
            jax.ShapeDtypeStruct((32, LZ * ZL), F32),
            jax.ShapeDtypeStruct((LZ * 4, 128), F32),
        ),
        in_specs=[hbm, hbm, hbm, hbm, hbm, vmem],
        out_specs=(vmem, vmem),
        scratch_shapes=[
            pltpu.SMEM((1, LZ), jnp.int32),
            pltpu.SMEM((SLOTS, LZ), jnp.int32),
            pltpu.VMEM((CHUNKS, 128), jnp.int32),
            pltpu.VMEM((CHUNKS, 128), F32),
            pltpu.VMEM((CHUNKS, 128), F32),
            pltpu.VMEM((CHUNKS, 128), F32),
            pltpu.VMEM((ROWS_ALL, SITE_DEV), F32),
            pltpu.VMEM((ROWS_ALL, SITE_DEV), BF16),
            pltpu.VMEM((CHUNKS * 16, 128), BF16),
            pltpu.VMEM((CHUNKS * 16, 256), F32),
            pltpu.VMEM((256, SITE_DEV), BF16),
            pltpu.VMEM((384, SITE_DEV), BF16),
            pltpu.VMEM((BUSES - 1, ROWS[0], PER), BF16),
            pltpu.VMEM((BUSES - 1, ROWS[1], PER), BF16),
            pltpu.VMEM((BUSES, ROWS[0], PER), BF16),
            pltpu.VMEM((BUSES, ROWS[1], PER), BF16),
            pltpu.VMEM((LZ, ZL, SLOTS * ZB), BF16),
            pltpu.VMEM((ZONES + 1, HALF, ZB), BF16),
            pltpu.VMEM((ZONES + 1, HALF, ZB), BF16),
            pltpu.VMEM((T, RING, RING, 16, ZL), BF16),
            pltpu.VMEM((T, 4, 2, 16, 256), BF16),
            pltpu.VMEM((T, 4, 4, 16, 256), BF16),
            pltpu.VMEM((T, 2, 4, 16, 256), BF16),
            pltpu.VMEM((T, 4, 16, 128), BF16),
            pltpu.VMEM((T, 4, 16, 256), BF16),
            pltpu.VMEM((48, 128), F32),
            pltpu.VMEM((BUSES, 48, 128), F32),
            dma((7,)),
            dma((LZ, SLOTS)),
            dma((2, BUSES)),
            dma((2, BUSES)),
            dma((len(GATHERS), 9)),
            dma((len(GATHERS), 9)),
            dma((T, 4)),
            dma((T, 4)),
            dma((len(SHARES), BUSES)),
            dma((len(SHARES), BUSES)),
        ],
        compiler_params=pltpu.CompilerParams(
            collective_id=0, has_side_effects=True, vmem_limit_bytes=62 * 1024 * 1024
        ),
        name="screen",
    )(
        block_count.T, block_zone.T, site_values, site_bus.reshape(-1, 128), ptdf_blocks,
        rating.reshape(-1, 128),
    )
    loading, worst = pl.pallas_call(
        hand_over,
        out_shape=(
            jax.ShapeDtypeStruct((32, LZ * ZL), F32),
            jax.ShapeDtypeStruct((LZ * 4, 128), F32),
        ),
        in_specs=[vmem, vmem],
        out_specs=(vmem, vmem),
        name="hand_over",
    )(loading, worst)
    return loading, worst.reshape(-1)


def solution(mesh):
    return jax.shard_map(
        body,
        mesh=mesh,
        in_specs=(
            P("line", "bus"),
            P(),
            P("line", "bus"),
            P("line", "bus"),
            P("line", "bus", None, None),
            P("line"),
        ),
        out_specs=(P("bus", "line"), P("line")),
        check_vma=False,
    )
```

```python
import functools

import jax
import jax.numpy as jnp
from jax import lax
from jax.experimental import pallas as pl
from jax.experimental.pallas import tpu as pltpu
from jax.sharding import PartitionSpec as P

MESH = pl.DeviceIdType.MESH
F32 = jnp.float32
BF16 = jnp.bfloat16

LINES = 8
BUSES = 16
RING = 4
BUS_DEV = 4480
SCEN_DEV = 64
SITE_DEV = 4096
PER = 256
ROWS = (48, 32)
ROWS_ALL = 80
DIGITS = 32
CHUNKS = SITE_DEV // 128
ZONES = 7
ZB = 640
LZ = 11
ZL = 512
SLOTS = 3
HALF = 256
T = 2 * LZ
DIRECT = 2
TR = T - DIRECT
NT = (((1,), (1,)), ((), ()))
LAG = (4, 8, 12, 16)
GATHER_AT = (4, 8)
GATHERS = ((0, 0, 3), (0, 3, 4), (1, 0, 7))
SHARES = (4, 8, 12)


def iota(shape, dim):
    return lax.broadcasted_iota(jnp.int32, shape, dim).astype(F32)


def kernel(
    count_hbm, zone_hbm, values_hbm, bus_hbm, blocks_hbm, rating_ref,
    load_ref, worst_ref,
    live_ref, slot_ref, ids, grp, hi, lo, raw, xa, g01, pre, bt, lhs, sv0, sv1, rv0, rv1, blk, inj0, inj1,
    flows, ra, rb, sa, rc, rd, rs, wl, wr,
    in_sem, blk_sem, xs_sem, xr_sem, gs_sem, gr_sem, fs_sem, fr_sem, ds_sem, dr_sem, ws_sem, wr_sem,
):
    line = lax.axis_index("line")
    bus = lax.axis_index("bus")
    y, core = line // 2, line % 2
    x, z = bus // RING, bus % RING
    up = ((y + 1) % RING) * 2 + core
    down = ((y + 3) % RING) * 2 + core
    sib = y * 2 + (1 - core)
    x1, x2, x3 = (x + 1) % RING, (x + 2) % RING, (x + 3) % RING
    z1, z2, z3 = (z + 1) % RING, (z + 2) % RING, (z + 3) % RING

    barrier = pltpu.get_barrier_semaphore()
    for j in range(1, BUSES):
        pl.semaphore_signal(barrier, inc=1, device_id=(line, (bus + j) % BUSES), device_id_type=MESH)
    for other in (up, down, sib):
        pl.semaphore_signal(barrier, inc=1, device_id=(other, bus), device_id_type=MESH)

    ids_copy = pltpu.make_async_copy(bus_hbm.at[pl.ds(bus * CHUNKS, CHUNKS)], ids, in_sem.at[0])
    ids_copy.start()
    val_copies = [
        pltpu.make_async_copy(values_hbm.at[pl.ds(16 * q, 16)], raw.at[pl.ds(row, 16)], in_sem.at[1 + q])
        for q, row in enumerate((0, 48, 16, 64))
    ]
    for copy in val_copies:
        copy.start()
    small_copies = [
        pltpu.make_async_copy(count_hbm, live_ref, in_sem.at[5]),
        pltpu.make_async_copy(zone_hbm, slot_ref, in_sem.at[6]),
    ]
    for copy in small_copies:
        copy.start()

    def block_copy(zone, slot):
        return pltpu.make_async_copy(
            blocks_hbm.at[zone, slot], blk.at[zone, :, pl.ds(slot * ZB, ZB)], blk_sem.at[zone, slot]
        )

    def start_blocks(zone, _):
        for slot in range(SLOTS):
            block_copy(zone, slot).start()
        return 0

    lax.fori_loop(0, LZ, start_blocks, 0)

    inj0[ZONES] = jnp.zeros((HALF, ZB), BF16)
    inj1[ZONES] = jnp.zeros((HALF, ZB), BF16)
    wl[...] = jnp.zeros_like(wl)
    ids_copy.wait()
    bus_ids = ids[...]
    group = jnp.zeros_like(bus_ids)
    for g in range(1, BUSES):
        group = group + (bus_ids >= g * BUS_DEV).astype(jnp.int32)
    offset = bus_ids - group * BUS_DEV
    grp[...] = group.astype(F32)
    hi[...] = (offset >> 8).astype(F32)
    lo[...] = (offset & 255).astype(F32)

    sub16 = iota((16, 128), 0)

    def lanes(c, width=128):
        return pl.ds(pl.multiple_of(c * width, width), width)

    def mark(c, _):
        row = grp[pl.ds(c, 1), :]
        g01[pl.ds(pl.multiple_of(c * 16, 16), 16), :] = jnp.where(row == sub16, 1.0, 0.0).astype(BF16)
        digits = jnp.where(sub16 == 0, hi[pl.ds(c, 1), :], jnp.where(sub16 == 1, lo[pl.ds(c, 1), :], 0.0))
        xa[pl.ds(DIGITS, 16), lanes(c)] = digits.astype(BF16)
        return 0

    lax.fori_loop(0, CHUNKS, mark, 0)
    ahead = lax.broadcasted_iota(jnp.int32, (128, 256), 0)
    place = lax.broadcasted_iota(jnp.int32, (128, 256), 1)
    steps = jnp.where((ahead <= place) | (place >= 128), 1.0, 0.0).astype(BF16)
    pre[...] = jnp.dot(g01[...], steps, preferred_element_type=F32)
    sub256 = iota((256, 128), 0)

    def rank(c, run):
        rows = pl.ds(pl.multiple_of(c * 16, 16), 16)
        counted = g01[rows, :].astype(F32) * (pre[rows, pl.ds(0, 128)] + run)
        position = jnp.sum(counted, axis=0, keepdims=True) - 1.0
        bt[:, lanes(c)] = jnp.where(position == sub256, 1.0, 0.0).astype(BF16)
        return run + pre[rows, pl.ds(128, 128)]

    lax.fori_loop(0, CHUNKS, rank, jnp.zeros((16, 128), F32))
    for copy in val_copies:
        copy.wait()

    def narrow(c, _):
        xa[pl.ds(0, 32), lanes(c)] = raw[pl.ds(0, 32), lanes(c)].astype(BF16)
        xa[pl.ds(48, 32), lanes(c)] = raw[pl.ds(48, 32), lanes(c)].astype(BF16)
        return 0

    lax.fori_loop(0, CHUNKS, narrow, 0)

    sv, rv = (sv0, sv1), (rv0, rv1)

    def chosen(row, value, vals):
        mask = jnp.where(jnp.broadcast_to(row, (16, row.shape[1])) == value, 1.0, 0.0).astype(BF16)
        return vals * jnp.concatenate([mask] * (vals.shape[0] // 16), axis=0)

    def pack(half):
        rows = ROWS[half]
        first = half * ROWS[0]
        for batch in range(2):
            owners = [(bus + batch * 8 + i + 1) % BUSES for i in range(8)]
            owners_f = [o.astype(F32) for o in owners]

            def pick(c, _):
                row = grp[pl.ds(c, 1), :]
                vals = xa[pl.ds(first, rows), lanes(c)]
                for i in range(8):
                    lhs[pl.ds(i * rows, rows), lanes(c)] = chosen(row, owners_f[i], vals)
                return 0

            lax.fori_loop(0, CHUNKS, pick, 0)
            packed = lax.dot_general(
                lhs[pl.ds(0, 8 * rows), :], bt[...], NT, preferred_element_type=F32
            ).astype(BF16)
            if half == 0 and batch == 0:
                pl.semaphore_wait(barrier, BUSES - 1 + 3)
            for i in range(8):
                j = batch * 8 + i
                if j < BUSES - 1:
                    sv[half][j] = packed[i * rows:(i + 1) * rows]
                    pltpu.make_async_remote_copy(
                        sv[half].at[j], rv[half].at[bus], xs_sem.at[half, j], xr_sem.at[half, bus],
                        device_id=(line, owners[i]), device_id_type=MESH,
                    ).start()
                else:
                    rv[half][bus] = packed[i * rows:(i + 1) * rows]

    def received(half):
        for j in range(1, BUSES):
            src = (bus + j) % BUSES
            pltpu.make_async_copy(rv[half].at[src], rv[half].at[src], xr_sem.at[half, src]).wait()

    def low_digit(k, _):
        row = rv0[k, pl.ds(DIGITS, 16), :].astype(F32)[1:2]
        bt[:, lanes(k, 256)] = jnp.where(row == iota((256, 256), 0), 1.0, 0.0).astype(BF16)
        return 0

    def spread(half, inj, after):
        for part in range(2):

            def high_digit(k, _):
                vals = rv[half][k, pl.ds(0, 32), :]
                row = rv0[k, pl.ds(DIGITS, 16), :].astype(F32)[0:1]
                for i in range(9):
                    lhs[pl.ds(i * 32, 32), lanes(k, 256)] = chosen(row, float(part * 9 + i), vals)
                return 0

            lax.fori_loop(0, BUSES, high_digit, 0)
            sums = lax.dot_general(
                lhs[pl.ds(0, 288), :], bt[...], NT, preferred_element_type=F32
            ).astype(BF16)
            for i in range(9):
                for t in range(2):
                    strip = 2 * (part * 9 + i) + t
                    if strip < ZONES * 5:
                        zone, lane = strip // 5, (strip % 5) * 128
                        inj[zone, pl.ds(pl.multiple_of(line * 32, 32), 32), lane:lane + 128] = sums[
                            i * 32:(i + 1) * 32, t * 128:t * 128 + 128
                        ]
            after[part]()

    def gathered(step, owner, first, count):
        half, zone, zones = GATHERS[step]
        rows = pl.ds(pl.multiple_of(owner * 32, 32) + first, count)
        return (inj1 if half else inj0).at[pl.ds(zone, zones), rows]

    def gather(step, number, owner, first, count, target):
        rows = gathered(step, owner, first, count)
        return pltpu.make_async_remote_copy(
            rows, rows, gs_sem.at[step, number], gr_sem.at[step, number],
            device_id=(target, bus), device_id_type=MESH,
        )

    def arrival(step, number, owner, first, count):
        rows = gathered(step, owner, first, count)
        return pltpu.make_async_copy(rows, rows, gr_sem.at[step, number])

    far = ((y + 2) % RING) * 2 + core
    sib_up = ((y + 1) % RING) * 2 + (1 - core)
    sib_down = ((y + 3) % RING) * 2 + (1 - core)
    sib_far = ((y + 2) % RING) * 2 + (1 - core)

    ROUTES = (
        (line, 0, 32, up),
        (line, 0, 32, down),
        (line, 0, 32, sib),
        (down, 0, 16, up),
        (down, 0, 32, sib),
        (up, 16, 16, down),
        (up, 0, 32, sib),
        (far, 0, 16, sib),
        (far, 16, 16, sib),
    )

    def route(step, number):
        return gather(step, number, *ROUTES[number])

    def gather_start(step):
        for number in range(3):
            route(step, number).start()

    def gather_relay(step):
        arrival(step, 0, down, 0, 32).wait()
        route(step, 3).start()
        route(step, 4).start()
        arrival(step, 1, up, 0, 32).wait()
        route(step, 5).start()
        route(step, 6).start()

    def gather_last(step):
        arrival(step, 3, far, 0, 16).wait()
        route(step, 7).start()
        arrival(step, 5, far, 16, 16).wait()
        route(step, 8).start()

    def gather_finish(step):
        arrival(step, 2, sib, 0, 32).wait()
        arrival(step, 4, sib_down, 0, 32).wait()
        arrival(step, 6, sib_up, 0, 32).wait()
        arrival(step, 7, sib_far, 0, 16).wait()
        arrival(step, 8, sib_far, 16, 16).wait()

    pack(0)
    pack(1)
    received(0)
    lax.fori_loop(0, BUSES, low_digit, 0)
    spread(0, inj0, (lambda: gather_start(0), lambda: gather_start(1)))
    received(1)
    spread(1, inj1, (lambda: gather_relay(0), lambda: gather_relay(1)))
    gather_start(2)
    for step in range(2):
        gather_last(step)
    for step in range(2):
        gather_finish(step)
    for copy in small_copies:
        copy.wait()

    A, B = pl.ds(0, 256), pl.ds(256, 256)
    L, R = pl.ds(0, 128), pl.ds(128, 128)
    LO, HI = pl.ds(0, 2), pl.ds(2, 2)
    ALL = pl.ds(0, 4)

    def push(src, dst, t, step, device):
        pltpu.make_async_remote_copy(
            src, dst, fs_sem.at[t, step], fr_sem.at[t, step],
            device_id=(line, device), device_id_type=MESH,
        ).start()

    xp, xm, zp, zm = x1 * RING + z, x3 * RING + z, x * RING + z1, x * RING + z3

    def add(a, b):
        return (a.astype(F32) + b.astype(F32)).astype(BF16)

    def add3(a, b, c):
        return a.astype(F32) + b.astype(F32) + c.astype(F32)

    def arrived(buf, t, step):
        pltpu.make_async_copy(buf.at[t], buf.at[t], fr_sem.at[t, step]).wait()

    def produce(t, zone, inj):
        live = live_ref[0, zone]
        pieces = []
        for slot in range(SLOTS):
            at = jnp.where(slot < live, slot_ref[slot, zone], ZONES)
            pieces.append(inj[at])
        out = lax.dot_general(
            jnp.concatenate(pieces, axis=1), blk[zone], NT, preferred_element_type=F32
        ).astype(BF16)

        def store():
            flows[t] = out.reshape(RING, RING, 16, ZL)

        def send():
            push(flows.at[t, x2, LO, :, A], ra.at[t, 0], t, 0, xp)
            push(flows.at[t, x2, HI, :, A], ra.at[t, 1], t, 0, xm)
            push(flows.at[t, LO, z2, :, B], ra.at[t, 2], t, 0, zp)
            push(flows.at[t, HI, z2, :, B], ra.at[t, 3], t, 0, zm)

        return store, send

    def first_b(t):
        sums = (
            add(flows[t, x1, LO, :, A], ra[t, 0]),
            add(flows[t, x3, HI, :, A], ra[t, 1]),
            add(flows[t, LO, z1, :, B], ra[t, 2]),
            add(flows[t, HI, z3, :, B], ra[t, 3]),
        )

        def store():
            flows[t, x1, LO, :, A] = sums[0]
            flows[t, x3, HI, :, A] = sums[1]
            flows[t, LO, z1, :, B] = sums[2]
            flows[t, HI, z3, :, B] = sums[3]

        def send():
            push(flows.at[t, x1, ALL, :, A], rb.at[t, 0], t, 1, xp)
            push(flows.at[t, x3, ALL, :, A], rb.at[t, 1], t, 1, xm)
            push(flows.at[t, ALL, z1, :, B], rb.at[t, 2], t, 1, zp)
            push(flows.at[t, ALL, z3, :, B], rb.at[t, 3], t, 1, zm)

        return store, send

    def second_a(t):
        sums = (
            add3(flows[t, x, ALL, :, A], rb[t, 0], rb[t, 1]).astype(BF16),
            add3(flows[t, ALL, z, :, B], rb[t, 2], rb[t, 3]).astype(BF16),
        )

        def store():
            sa[t, 0] = sums[0]
            sa[t, 1] = sums[1]

        def send():
            push(sa.at[t, 0, z2, :, L], rc.at[t, 0], t, 2, zp)
            push(sa.at[t, 0, z2, :, R], rc.at[t, 1], t, 2, zm)
            push(sa.at[t, 1, x2, :, L], rc.at[t, 2], t, 2, xp)
            push(sa.at[t, 1, x2, :, R], rc.at[t, 3], t, 2, xm)

        return store, send

    def second_b(t):
        sums = (
            add(sa[t, 0, z1, :, L], rc[t, 0]),
            add(sa[t, 0, z3, :, R], rc[t, 1]),
            add(sa[t, 1, x1, :, L], rc[t, 2]),
            add(sa[t, 1, x3, :, R], rc[t, 3]),
        )

        def store():
            sa[t, 0, z1, :, L] = sums[0]
            sa[t, 0, z3, :, R] = sums[1]
            sa[t, 1, x1, :, L] = sums[2]
            sa[t, 1, x3, :, R] = sums[3]

        def send():
            push(sa.at[t, 0, z1], rd.at[t, 0], t, 3, zp)
            push(sa.at[t, 0, z3], rd.at[t, 1], t, 3, zm)
            push(sa.at[t, 1, x1], rd.at[t, 2], t, 3, xp)
            push(sa.at[t, 1, x3], rd.at[t, 3], t, 3, xm)

        return store, send

    def settle(t, flow):
        zone, half = t % LZ, t // LZ
        ratings = jnp.concatenate([rating_ref[pl.ds(zone * 4 + i, 1), :] for i in range(4)], axis=1)
        loading = flow / ratings
        top = jnp.max(jnp.abs(loading), axis=0, keepdims=True)
        start = half * 16 if isinstance(half, int) else pl.multiple_of(half * 16, 16)
        left = zone * ZL if isinstance(zone, int) else pl.multiple_of(zone * ZL, ZL)
        load_ref[pl.ds(start, 16), pl.ds(left, ZL)] = loading
        for i in range(4):
            row = pl.ds(zone * 4 + i, 1)
            wl[row, :] = jnp.maximum(wl[row, :], top[:, i * 128:(i + 1) * 128])

    def finish(t):
        flow = jnp.concatenate(
            [add3(sa[t, 0, z], rd[t, 0], rd[t, 1]), add3(sa[t, 1, x], rd[t, 2], rd[t, 3])], axis=1
        )

        def store():
            settle(t, flow)

        def send():
            for step, buf in enumerate((ra, rb, rc, rd)):
                pltpu.make_async_copy(buf.at[t], buf.at[t], fs_sem.at[t, step]).wait()

        return store, send

    parts = [pl.ds(first * 4, (last - first) * 4) for first, last in zip((0, *SHARES), SHARES)]

    def share(part):
        for j in range(1, BUSES):
            pltpu.make_async_remote_copy(
                wl.at[parts[part]], wr.at[bus, parts[part]], ws_sem.at[part, j], wr_sem.at[part, bus],
                device_id=(line, (bus + j) % BUSES), device_id_type=MESH,
            ).start()

    STEPS = tuple(zip((first_b, second_a, second_b, finish), (ra, rb, rc, rd), LAG))

    def straight(t):
        for j in range(1, BUSES):
            owner = (bus + j) % BUSES
            pltpu.make_async_remote_copy(
                flows.at[t, owner // RING, owner % RING], rs.at[t - TR, bus], ds_sem.at[t - TR, j], dr_sem.at[t - TR, bus],
                device_id=(line, owner), device_id_type=MESH,
            ).start()

    def straight_finish(t):
        flow = flows[t, x, z].astype(F32)
        for j in range(1, BUSES):
            src = rs.at[t - TR, (bus + j) % BUSES]
            pltpu.make_async_copy(src, src, dr_sem.at[t - TR, (bus + j) % BUSES]).wait()
        for j in range(1, BUSES):
            flow = flow + rs[t - TR, (bus + j) % BUSES].astype(F32)
        settle(t, flow)

    def iteration(active, produces, t):
        if produces:
            if produces == 1:
                for slot in range(SLOTS):
                    block_copy(t, slot).wait()
            store, send = produce(t, t % LZ, inj0 if produces == 1 else inj1)
            store()
            if produces == 3:
                straight(t)
            else:
                send()
        for step in active:
            arrived(STEPS[step][1], t - STEPS[step][2], step)
            store, send = STEPS[step][0](t - STEPS[step][2])
            store()
            send()

    before = {GATHER_AT[0]: [lambda: gather_relay(2)], GATHER_AT[1]: [lambda: gather_last(2)], LZ: [lambda: gather_finish(2)]}
    for part in range(len(parts) - 1):
        before.setdefault(LAG[3] + LZ + SHARES[part], []).append(functools.partial(share, part))
    for t in range(TR, T):
        before.setdefault(TR + LAG[3] - 1, []).append(functools.partial(straight_finish, t))
    edges = sorted({0, LZ, TR, T, TR + LAG[3], *LAG, *(TR + lag for lag in LAG), *before})
    for first, last in zip(edges, edges[1:]):
        for hook in before.get(first, ()):
            hook()
        active = [step for step in range(4) if LAG[step] <= first < TR + LAG[step]]
        produces = 0 if first >= T else 3 if first >= TR else 2 if first >= LZ else 1

        def run(t, _, active=active, produces=produces):
            iteration(active, produces, t)
            return 0

        lax.fori_loop(first, last, run, 0)

    share(len(parts) - 1)
    for t in range(TR, T):
        for j in range(1, BUSES):
            src = rs.at[t - TR, 0]
            pltpu.make_async_copy(src, src, ds_sem.at[t - TR, j]).wait()
    for step in range(len(GATHERS)):
        for number in range(len(ROUTES)):
            route(step, number).wait_send()
    for half in range(2):
        for j in range(BUSES - 1):
            pltpu.make_async_copy(sv[half].at[j], sv[half].at[j], xs_sem.at[half, j]).wait()
    best = wl[...]
    for part in range(len(parts)):
        for j in range(1, BUSES):
            src = wr.at[(bus + j) % BUSES, parts[part]]
            pltpu.make_async_copy(src, src, wr_sem.at[part, (bus + j) % BUSES]).wait()
    for j in range(1, BUSES):
        best = jnp.maximum(best, wr[(bus + j) % BUSES])
    worst_ref[...] = best[0:LZ * 4]
    for part in range(len(parts)):
        for j in range(1, BUSES):
            src = wl.at[parts[part]]
            pltpu.make_async_copy(src, src, ws_sem.at[part, j]).wait()


def hand_over(load_in, worst_in, load_ref, worst_ref):
    load_ref[...] = load_in[...]
    worst_ref[...] = worst_in[...]


def body(site_values, site_bus, block_count, block_zone, ptdf_blocks, rating):
    hbm = pl.BlockSpec(memory_space=pl.ANY)
    vmem = pl.BlockSpec(memory_space=pltpu.VMEM)
    dma = pltpu.SemaphoreType.DMA
    loading, worst = pl.pallas_call(
        kernel,
        out_shape=(
            jax.ShapeDtypeStruct((32, LZ * ZL), F32),
            jax.ShapeDtypeStruct((LZ * 4, 128), F32),
        ),
        in_specs=[hbm, hbm, hbm, hbm, hbm, vmem],
        out_specs=(vmem, vmem),
        scratch_shapes=[
            pltpu.SMEM((1, LZ), jnp.int32),
            pltpu.SMEM((SLOTS, LZ), jnp.int32),
            pltpu.VMEM((CHUNKS, 128), jnp.int32),
            pltpu.VMEM((CHUNKS, 128), F32),
            pltpu.VMEM((CHUNKS, 128), F32),
            pltpu.VMEM((CHUNKS, 128), F32),
            pltpu.VMEM((ROWS_ALL, SITE_DEV), F32),
            pltpu.VMEM((ROWS_ALL, SITE_DEV), BF16),
            pltpu.VMEM((CHUNKS * 16, 128), BF16),
            pltpu.VMEM((CHUNKS * 16, 256), F32),
            pltpu.VMEM((256, SITE_DEV), BF16),
            pltpu.VMEM((384, SITE_DEV), BF16),
            pltpu.VMEM((BUSES - 1, ROWS[0], PER), BF16),
            pltpu.VMEM((BUSES - 1, ROWS[1], PER), BF16),
            pltpu.VMEM((BUSES, ROWS[0], PER), BF16),
            pltpu.VMEM((BUSES, ROWS[1], PER), BF16),
            pltpu.VMEM((LZ, ZL, SLOTS * ZB), BF16),
            pltpu.VMEM((ZONES + 1, HALF, ZB), BF16),
            pltpu.VMEM((ZONES + 1, HALF, ZB), BF16),
            pltpu.VMEM((T, RING, RING, 16, ZL), BF16),
            pltpu.VMEM((TR, 4, 2, 16, 256), BF16),
            pltpu.VMEM((TR, 4, 4, 16, 256), BF16),
            pltpu.VMEM((TR, 2, 4, 16, 256), BF16),
            pltpu.VMEM((TR, 4, 16, 128), BF16),
            pltpu.VMEM((TR, 4, 16, 256), BF16),
            pltpu.VMEM((DIRECT, BUSES, 16, ZL), BF16),
            pltpu.VMEM((48, 128), F32),
            pltpu.VMEM((BUSES, 48, 128), F32),
            dma((7,)),
            dma((LZ, SLOTS)),
            dma((2, BUSES)),
            dma((2, BUSES)),
            dma((len(GATHERS), 9)),
            dma((len(GATHERS), 9)),
            dma((TR, 4)),
            dma((TR, 4)),
            dma((DIRECT, BUSES)),
            dma((DIRECT, BUSES)),
            dma((len(SHARES), BUSES)),
            dma((len(SHARES), BUSES)),
        ],
        compiler_params=pltpu.CompilerParams(
            collective_id=0, has_side_effects=True, vmem_limit_bytes=62 * 1024 * 1024
        ),
        name="screen",
    )(
        block_count.T, block_zone.T, site_values, site_bus.reshape(-1, 128), ptdf_blocks,
        rating.reshape(-1, 128),
    )
    loading, worst = pl.pallas_call(
        hand_over,
        out_shape=(
            jax.ShapeDtypeStruct((32, LZ * ZL), F32),
            jax.ShapeDtypeStruct((LZ * 4, 128), F32),
        ),
        in_specs=[vmem, vmem],
        out_specs=(vmem, vmem),
        name="hand_over",
    )(loading, worst)
    return loading, worst.reshape(-1)


def solution(mesh):
    return jax.shard_map(
        body,
        mesh=mesh,
        in_specs=(
            P("line", "bus"),
            P(),
            P("line", "bus"),
            P("line", "bus"),
            P("line", "bus", None, None),
            P("line"),
        ),
        out_specs=(P("bus", "line"), P("line")),
        check_vma=False,
    )
```

```python
import functools

import jax
import jax.numpy as jnp
from jax import lax
from jax.experimental import pallas as pl
from jax.experimental.pallas import tpu as pltpu
from jax.sharding import PartitionSpec as P

MESH = pl.DeviceIdType.MESH
F32 = jnp.float32
BF16 = jnp.bfloat16

LINES = 8
BUSES = 16
RING = 4
BUS_DEV = 4480
SCEN_DEV = 64
SITE_DEV = 4096
PER = 256
ROWS = (48, 32)
ROWS_ALL = 80
DIGITS = 32
CHUNKS = SITE_DEV // 128
ZONES = 7
ZB = 640
LZ = 11
ZL = 512
SLOTS = 3
HALF = 256
T = 2 * LZ
NT = (((1,), (1,)), ((), ()))
LAG = (4, 8, 12, 16)
GATHERS = ((0, 0, 3), (0, 3, 2), (0, 5, 1), (0, 6, 1), (1, 0, 7))
SHARES = (4, 8, 10, 12)


def iota(shape, dim):
    return lax.broadcasted_iota(jnp.int32, shape, dim).astype(F32)


def kernel(
    count_hbm, zone_hbm, values_hbm, bus_hbm, blocks_hbm, rating_ref,
    load_hbm, worst_ref,
    live_ref, slot_ref, ids, grp, hi, lo, raw, xa, g01, pre, bt, lhs, sv0, sv1, rv0, rv1, blk, inj0, inj1,
    flows, ra, rb, sa, rc, rd, load_ref, wl, wr,
    in_sem, blk_sem, xs_sem, xr_sem, gs_sem, gr_sem, fs_sem, fr_sem, ws_sem, wr_sem, out_sem,
):
    line = lax.axis_index("line")
    bus = lax.axis_index("bus")
    y, core = line // 2, line % 2
    x, z = bus // RING, bus % RING
    up = ((y + 1) % RING) * 2 + core
    down = ((y + 3) % RING) * 2 + core
    sib = y * 2 + (1 - core)
    x1, x2, x3 = (x + 1) % RING, (x + 2) % RING, (x + 3) % RING
    z1, z2, z3 = (z + 1) % RING, (z + 2) % RING, (z + 3) % RING

    barrier = pltpu.get_barrier_semaphore()
    for j in range(1, BUSES):
        pl.semaphore_signal(barrier, inc=1, device_id=(line, (bus + j) % BUSES), device_id_type=MESH)
    for other in (up, down, sib):
        pl.semaphore_signal(barrier, inc=1, device_id=(other, bus), device_id_type=MESH)

    ids_copy = pltpu.make_async_copy(bus_hbm.at[pl.ds(bus * CHUNKS, CHUNKS)], ids, in_sem.at[0])
    ids_copy.start()
    val_copies = [
        pltpu.make_async_copy(values_hbm.at[pl.ds(16 * q, 16)], raw.at[pl.ds(row, 16)], in_sem.at[1 + q])
        for q, row in enumerate((0, 48, 16, 64))
    ]
    for copy in val_copies:
        copy.start()
    small_copies = [
        pltpu.make_async_copy(count_hbm, live_ref, in_sem.at[5]),
        pltpu.make_async_copy(zone_hbm, slot_ref, in_sem.at[6]),
    ]
    for copy in small_copies:
        copy.start()

    def block_copy(zone, slot):
        return pltpu.make_async_copy(
            blocks_hbm.at[zone, slot], blk.at[zone, :, pl.ds(slot * ZB, ZB)], blk_sem.at[zone, slot]
        )

    def start_blocks(zone, _):
        for slot in range(SLOTS):
            block_copy(zone, slot).start()
        return 0

    lax.fori_loop(0, LZ, start_blocks, 0)

    inj0[ZONES] = jnp.zeros((HALF, ZB), BF16)
    inj1[ZONES] = jnp.zeros((HALF, ZB), BF16)
    wl[...] = jnp.zeros_like(wl)
    ids_copy.wait()
    bus_ids = ids[...]
    group = jnp.zeros_like(bus_ids)
    for g in range(1, BUSES):
        group = group + (bus_ids >= g * BUS_DEV).astype(jnp.int32)
    offset = bus_ids - group * BUS_DEV
    grp[...] = group.astype(F32)
    hi[...] = (offset >> 8).astype(F32)
    lo[...] = (offset & 255).astype(F32)

    sub16 = iota((16, 128), 0)

    def lanes(c, width=128):
        return pl.ds(pl.multiple_of(c * width, width), width)

    def mark(c, _):
        row = grp[pl.ds(c, 1), :]
        g01[pl.ds(pl.multiple_of(c * 16, 16), 16), :] = jnp.where(row == sub16, 1.0, 0.0).astype(BF16)
        digits = jnp.where(sub16 == 0, hi[pl.ds(c, 1), :], jnp.where(sub16 == 1, lo[pl.ds(c, 1), :], 0.0))
        xa[pl.ds(DIGITS, 16), lanes(c)] = digits.astype(BF16)
        return 0

    lax.fori_loop(0, CHUNKS, mark, 0)
    ahead = lax.broadcasted_iota(jnp.int32, (128, 256), 0)
    place = lax.broadcasted_iota(jnp.int32, (128, 256), 1)
    steps = jnp.where((ahead <= place) | (place >= 128), 1.0, 0.0).astype(BF16)
    pre[...] = jnp.dot(g01[...], steps, preferred_element_type=F32)
    sub256 = iota((256, 128), 0)

    def rank(c, run):
        rows = pl.ds(pl.multiple_of(c * 16, 16), 16)
        counted = g01[rows, :].astype(F32) * (pre[rows, pl.ds(0, 128)] + run)
        position = jnp.sum(counted, axis=0, keepdims=True) - 1.0
        bt[:, lanes(c)] = jnp.where(position == sub256, 1.0, 0.0).astype(BF16)
        return run + pre[rows, pl.ds(128, 128)]

    lax.fori_loop(0, CHUNKS, rank, jnp.zeros((16, 128), F32))
    for copy in val_copies:
        copy.wait()

    def narrow(c, _):
        xa[pl.ds(0, 32), lanes(c)] = raw[pl.ds(0, 32), lanes(c)].astype(BF16)
        xa[pl.ds(48, 32), lanes(c)] = raw[pl.ds(48, 32), lanes(c)].astype(BF16)
        return 0

    lax.fori_loop(0, CHUNKS, narrow, 0)

    sv, rv = (sv0, sv1), (rv0, rv1)

    def chosen(row, value, vals):
        mask = jnp.where(jnp.broadcast_to(row, (16, row.shape[1])) == value, 1.0, 0.0).astype(BF16)
        return vals * jnp.concatenate([mask] * (vals.shape[0] // 16), axis=0)

    def pack(half):
        rows = ROWS[half]
        first = half * ROWS[0]
        for batch in range(2):
            owners = [(bus + batch * 8 + i + 1) % BUSES for i in range(8)]
            owners_f = [o.astype(F32) for o in owners]

            def pick(c, _):
                row = grp[pl.ds(c, 1), :]
                vals = xa[pl.ds(first, rows), lanes(c)]
                for i in range(8):
                    lhs[pl.ds(i * rows, rows), lanes(c)] = chosen(row, owners_f[i], vals)
                return 0

            lax.fori_loop(0, CHUNKS, pick, 0)
            packed = lax.dot_general(
                lhs[pl.ds(0, 8 * rows), :], bt[...], NT, preferred_element_type=F32
            ).astype(BF16)
            if half == 0 and batch == 0:
                pl.semaphore_wait(barrier, BUSES - 1 + 3)
            for i in range(8):
                j = batch * 8 + i
                if j < BUSES - 1:
                    sv[half][j] = packed[i * rows:(i + 1) * rows]
                    pltpu.make_async_remote_copy(
                        sv[half].at[j], rv[half].at[bus], xs_sem.at[half, j], xr_sem.at[half, bus],
                        device_id=(line, owners[i]), device_id_type=MESH,
                    ).start()
                else:
                    rv[half][bus] = packed[i * rows:(i + 1) * rows]

    def received(half):
        for j in range(1, BUSES):
            src = (bus + j) % BUSES
            pltpu.make_async_copy(rv[half].at[src], rv[half].at[src], xr_sem.at[half, src]).wait()

    def low_digit(k, _):
        row = rv0[k, pl.ds(DIGITS, 16), :].astype(F32)[1:2]
        bt[:, lanes(k, 256)] = jnp.where(row == iota((256, 256), 0), 1.0, 0.0).astype(BF16)
        return 0

    def spread(half, inj, after):
        for part in range(2):

            def high_digit(k, _):
                vals = rv[half][k, pl.ds(0, 32), :]
                row = rv0[k, pl.ds(DIGITS, 16), :].astype(F32)[0:1]
                for i in range(9):
                    lhs[pl.ds(i * 32, 32), lanes(k, 256)] = chosen(row, float(part * 9 + i), vals)
                return 0

            lax.fori_loop(0, BUSES, high_digit, 0)
            sums = lax.dot_general(
                lhs[pl.ds(0, 288), :], bt[...], NT, preferred_element_type=F32
            ).astype(BF16)
            for i in range(9):
                for t in range(2):
                    strip = 2 * (part * 9 + i) + t
                    if strip < ZONES * 5:
                        zone, lane = strip // 5, (strip % 5) * 128
                        inj[zone, pl.ds(pl.multiple_of(line * 32, 32), 32), lane:lane + 128] = sums[
                            i * 32:(i + 1) * 32, t * 128:t * 128 + 128
                        ]
            after[part]()

    def gathered(step, owner, first, count):
        half, zone, zones = GATHERS[step]
        rows = pl.ds(pl.multiple_of(owner * 32, 32) + first, count)
        return (inj1 if half else inj0).at[pl.ds(zone, zones), rows]

    def gather(step, number, owner, first, count, target):
        rows = gathered(step, owner, first, count)
        return pltpu.make_async_remote_copy(
            rows, rows, gs_sem.at[step, number], gr_sem.at[step, number],
            device_id=(target, bus), device_id_type=MESH,
        )

    def arrival(step, number, owner, first, count):
        rows = gathered(step, owner, first, count)
        return pltpu.make_async_copy(rows, rows, gr_sem.at[step, number])

    far = ((y + 2) % RING) * 2 + core
    sib_up = ((y + 1) % RING) * 2 + (1 - core)
    sib_down = ((y + 3) % RING) * 2 + (1 - core)
    sib_far = ((y + 2) % RING) * 2 + (1 - core)

    ROUTES = (
        (line, 0, 32, up),
        (line, 0, 32, down),
        (line, 0, 32, sib),
        (down, 0, 16, up),
        (down, 0, 32, sib),
        (up, 16, 16, down),
        (up, 0, 32, sib),
        (far, 0, 16, sib),
        (far, 16, 16, sib),
    )

    def route(step, number):
        return gather(step, number, *ROUTES[number])

    def gather_start(step):
        for number in range(3):
            route(step, number).start()

    def gather_relay(step):
        arrival(step, 0, down, 0, 32).wait()
        route(step, 3).start()
        route(step, 4).start()
        arrival(step, 1, up, 0, 32).wait()
        route(step, 5).start()
        route(step, 6).start()

    def gather_last(step):
        arrival(step, 3, far, 0, 16).wait()
        route(step, 7).start()
        arrival(step, 5, far, 16, 16).wait()
        route(step, 8).start()

    def gather_finish(step):
        arrival(step, 2, sib, 0, 32).wait()
        arrival(step, 4, sib_down, 0, 32).wait()
        arrival(step, 6, sib_up, 0, 32).wait()
        arrival(step, 7, sib_far, 0, 16).wait()
        arrival(step, 8, sib_far, 16, 16).wait()

    pack(0)
    pack(1)
    received(0)
    lax.fori_loop(0, BUSES, low_digit, 0)
    early = range(1, len(GATHERS) - 1)
    late = len(GATHERS) - 1

    def each(stage, steps):
        for step in steps:
            stage(step)

    spread(0, inj0, (lambda: gather_start(0), lambda: each(gather_start, early)))
    received(1)
    spread(1, inj1, (lambda: gather_relay(0), lambda: each(gather_relay, early)))
    gather_start(late)
    each(gather_last, range(late))
    each(gather_finish, range(late))
    for copy in small_copies:
        copy.wait()

    A, B = pl.ds(0, 256), pl.ds(256, 256)
    L, R = pl.ds(0, 128), pl.ds(128, 128)
    LO, HI = pl.ds(0, 2), pl.ds(2, 2)
    ALL = pl.ds(0, 4)

    def push(src, dst, t, step, device):
        pltpu.make_async_remote_copy(
            src, dst, fs_sem.at[t, step], fr_sem.at[t, step],
            device_id=(line, device), device_id_type=MESH,
        ).start()

    xp, xm, zp, zm = x1 * RING + z, x3 * RING + z, x * RING + z1, x * RING + z3

    def produce(t, zone, inj):
        for slot in range(SLOTS):
            @pl.when(t < LZ)
            def _():
                block_copy(zone, slot).wait()
        live = live_ref[0, zone]
        pieces = []
        for slot in range(SLOTS):
            at = jnp.where(slot < live, slot_ref[slot, zone], ZONES)
            pieces.append(inj[at])
        out = lax.dot_general(
            jnp.concatenate(pieces, axis=1), blk[zone], NT, preferred_element_type=F32
        ).astype(BF16)
        flows[t] = out.reshape(RING, RING, 16, ZL)
        push(flows.at[t, x2, LO, :, A], ra.at[t, 0], t, 0, xp)
        push(flows.at[t, x2, HI, :, A], ra.at[t, 1], t, 0, xm)
        push(flows.at[t, LO, z2, :, B], ra.at[t, 2], t, 0, zp)
        push(flows.at[t, HI, z2, :, B], ra.at[t, 3], t, 0, zm)

    def arrived(buf, t, step):
        pltpu.make_async_copy(buf.at[t], buf.at[t], fr_sem.at[t, step]).wait()

    def add(a, b):
        return (a.astype(F32) + b.astype(F32)).astype(BF16)

    def first_b(t):
        arrived(ra, t, 0)
        sums = (
            add(flows[t, x1, LO, :, A], ra[t, 0]),
            add(flows[t, x3, HI, :, A], ra[t, 1]),
            add(flows[t, LO, z1, :, B], ra[t, 2]),
            add(flows[t, HI, z3, :, B], ra[t, 3]),
        )
        flows[t, x1, LO, :, A] = sums[0]
        flows[t, x3, HI, :, A] = sums[1]
        flows[t, LO, z1, :, B] = sums[2]
        flows[t, HI, z3, :, B] = sums[3]
        push(flows.at[t, x1, ALL, :, A], rb.at[t, 0], t, 1, xp)
        push(flows.at[t, x3, ALL, :, A], rb.at[t, 1], t, 1, xm)
        push(flows.at[t, ALL, z1, :, B], rb.at[t, 2], t, 1, zp)
        push(flows.at[t, ALL, z3, :, B], rb.at[t, 3], t, 1, zm)

    def add3(a, b, c):
        return a.astype(F32) + b.astype(F32) + c.astype(F32)

    def second_a(t):
        arrived(rb, t, 1)
        sums = (
            add3(flows[t, x, ALL, :, A], rb[t, 0], rb[t, 1]).astype(BF16),
            add3(flows[t, ALL, z, :, B], rb[t, 2], rb[t, 3]).astype(BF16),
        )
        sa[t, 0] = sums[0]
        sa[t, 1] = sums[1]
        push(sa.at[t, 0, z2, :, L], rc.at[t, 0], t, 2, zp)
        push(sa.at[t, 0, z2, :, R], rc.at[t, 1], t, 2, zm)
        push(sa.at[t, 1, x2, :, L], rc.at[t, 2], t, 2, xp)
        push(sa.at[t, 1, x2, :, R], rc.at[t, 3], t, 2, xm)

    def second_b(t):
        arrived(rc, t, 2)
        sums = (
            add(sa[t, 0, z1, :, L], rc[t, 0]),
            add(sa[t, 0, z3, :, R], rc[t, 1]),
            add(sa[t, 1, x1, :, L], rc[t, 2]),
            add(sa[t, 1, x3, :, R], rc[t, 3]),
        )
        sa[t, 0, z1, :, L] = sums[0]
        sa[t, 0, z3, :, R] = sums[1]
        sa[t, 1, x1, :, L] = sums[2]
        sa[t, 1, x3, :, R] = sums[3]
        push(sa.at[t, 0, z1], rd.at[t, 0], t, 3, zp)
        push(sa.at[t, 0, z3], rd.at[t, 1], t, 3, zm)
        push(sa.at[t, 1, x1], rd.at[t, 2], t, 3, xp)
        push(sa.at[t, 1, x3], rd.at[t, 3], t, 3, xm)

    def leave(t, zone, half):
        part = (pl.ds(pl.multiple_of(half * 16, 16), 16), lanes(zone, ZL))
        return pltpu.make_async_copy(load_ref.at[part], load_hbm.at[part], out_sem.at[t])

    def finish(t, zone, half):
        arrived(rd, t, 3)
        ratings = jnp.concatenate([rating_ref[pl.ds(zone * 4 + i, 1), :] for i in range(4)], axis=1)
        flow = jnp.concatenate(
            [add3(sa[t, 0, z], rd[t, 0], rd[t, 1]), add3(sa[t, 1, x], rd[t, 2], rd[t, 3])], axis=1
        )
        loading = flow / ratings
        load_ref[pl.ds(pl.multiple_of(half * 16, 16), 16), lanes(zone, ZL)] = loading
        leave(t, zone, half).start()
        top = jnp.max(jnp.abs(loading), axis=0, keepdims=True)
        for i in range(4):
            row = pl.ds(zone * 4 + i, 1)
            wl[row, :] = jnp.maximum(wl[row, :], top[:, i * 128:(i + 1) * 128])
        for step, buf in enumerate((ra, rb, rc, rd)):
            pltpu.make_async_copy(buf.at[t], buf.at[t], fs_sem.at[t, step]).wait()

    parts = [pl.ds(first * 4, (last - first) * 4) for first, last in zip((0, *SHARES), SHARES)]

    def share(part):
        for j in range(1, BUSES):
            pltpu.make_async_remote_copy(
                wl.at[parts[part]], wr.at[bus, parts[part]], ws_sem.at[part, j], wr_sem.at[part, bus],
                device_id=(line, (bus + j) % BUSES), device_id_type=MESH,
            ).start()

    def stages(t):
        d1, d2, d3, d4 = LAG

        def when(lag, stage):
            @pl.when((t >= lag) & (t < T + lag))
            def _():
                stage(t - lag)

        when(d1, first_b)
        when(d2, second_a)
        when(d3, second_b)

        @pl.when((t >= d4) & (t < T + d4))
        def _():
            finish(t - d4, (t - d4) % LZ, (t - d4) // LZ)

        for part in range(len(parts) - 1):
            @pl.when(t == d4 + LZ + SHARES[part] - 1)
            def _(part=part):
                share(part)

    def first_half(t, _):
        produce(t, t, inj0)

        @pl.when(t == 4)
        def _():
            gather_relay(late)

        @pl.when(t == 8)
        def _():
            gather_last(late)

        stages(t)
        return 0

    def second_half(t, _):
        produce(t, t - LZ, inj1)
        stages(t)
        return 0

    def drain(t, _):
        stages(t)
        return 0

    lax.fori_loop(0, LZ, first_half, 0)
    gather_finish(late)
    lax.fori_loop(LZ, T, second_half, 0)
    lax.fori_loop(T, T + LAG[3], drain, 0)

    share(len(parts) - 1)
    for step in range(len(GATHERS)):
        for number in range(len(ROUTES)):
            route(step, number).wait_send()
    for half in range(2):
        for j in range(BUSES - 1):
            pltpu.make_async_copy(sv[half].at[j], sv[half].at[j], xs_sem.at[half, j]).wait()

    def gone(t, _):
        leave(t, t % LZ, t // LZ).wait()
        return 0

    lax.fori_loop(0, T, gone, 0)
    best = wl[...]
    for part in range(len(parts)):
        for j in range(1, BUSES):
            src = wr.at[(bus + j) % BUSES, parts[part]]
            pltpu.make_async_copy(src, src, wr_sem.at[part, (bus + j) % BUSES]).wait()
    for j in range(1, BUSES):
        best = jnp.maximum(best, wr[(bus + j) % BUSES])
    worst_ref[...] = best[0:LZ * 4]
    for part in range(len(parts)):
        for j in range(1, BUSES):
            src = wl.at[parts[part]]
            pltpu.make_async_copy(src, src, ws_sem.at[part, j]).wait()


def hand_over(load_in, worst_in, load_ref, worst_ref):
    load_ref[...] = load_in[...]
    worst_ref[...] = worst_in[...]


def body(site_values, site_bus, block_count, block_zone, ptdf_blocks, rating):
    hbm = pl.BlockSpec(memory_space=pl.ANY)
    vmem = pl.BlockSpec(memory_space=pltpu.VMEM)
    dma = pltpu.SemaphoreType.DMA
    loading, worst = pl.pallas_call(
        kernel,
        out_shape=(
            jax.ShapeDtypeStruct((32, LZ * ZL), F32),
            jax.ShapeDtypeStruct((LZ * 4, 128), F32),
        ),
        in_specs=[hbm, hbm, hbm, hbm, hbm, vmem],
        out_specs=(hbm, vmem),
        scratch_shapes=[
            pltpu.SMEM((1, LZ), jnp.int32),
            pltpu.SMEM((SLOTS, LZ), jnp.int32),
            pltpu.VMEM((CHUNKS, 128), jnp.int32),
            pltpu.VMEM((CHUNKS, 128), F32),
            pltpu.VMEM((CHUNKS, 128), F32),
            pltpu.VMEM((CHUNKS, 128), F32),
            pltpu.VMEM((ROWS_ALL, SITE_DEV), F32),
            pltpu.VMEM((ROWS_ALL, SITE_DEV), BF16),
            pltpu.VMEM((CHUNKS * 16, 128), BF16),
            pltpu.VMEM((CHUNKS * 16, 256), F32),
            pltpu.VMEM((256, SITE_DEV), BF16),
            pltpu.VMEM((384, SITE_DEV), BF16),
            pltpu.VMEM((BUSES - 1, ROWS[0], PER), BF16),
            pltpu.VMEM((BUSES - 1, ROWS[1], PER), BF16),
            pltpu.VMEM((BUSES, ROWS[0], PER), BF16),
            pltpu.VMEM((BUSES, ROWS[1], PER), BF16),
            pltpu.VMEM((LZ, ZL, SLOTS * ZB), BF16),
            pltpu.VMEM((ZONES + 1, HALF, ZB), BF16),
            pltpu.VMEM((ZONES + 1, HALF, ZB), BF16),
            pltpu.VMEM((T, RING, RING, 16, ZL), BF16),
            pltpu.VMEM((T, 4, 2, 16, 256), BF16),
            pltpu.VMEM((T, 4, 4, 16, 256), BF16),
            pltpu.VMEM((T, 2, 4, 16, 256), BF16),
            pltpu.VMEM((T, 4, 16, 128), BF16),
            pltpu.VMEM((T, 4, 16, 256), BF16),
            pltpu.VMEM((32, LZ * ZL), F32),
            pltpu.VMEM((48, 128), F32),
            pltpu.VMEM((BUSES, 48, 128), F32),
            dma((7,)),
            dma((LZ, SLOTS)),
            dma((2, BUSES)),
            dma((2, BUSES)),
            dma((len(GATHERS), 9)),
            dma((len(GATHERS), 9)),
            dma((T, 4)),
            dma((T, 4)),
            dma((len(SHARES), BUSES)),
            dma((len(SHARES), BUSES)),
            dma((T,)),
        ],
        compiler_params=pltpu.CompilerParams(
            collective_id=0, has_side_effects=True, vmem_limit_bytes=62 * 1024 * 1024
        ),
        name="screen",
    )(
        block_count.T, block_zone.T, site_values, site_bus.reshape(-1, 128), ptdf_blocks,
        rating.reshape(-1, 128),
    )
    loading, worst = pl.pallas_call(
        hand_over,
        out_shape=(
            jax.ShapeDtypeStruct((32, LZ * ZL), F32),
            jax.ShapeDtypeStruct((LZ * 4, 128), F32),
        ),
        in_specs=[vmem, vmem],
        out_specs=(vmem, vmem),
        name="hand_over",
    )(loading, worst)
    return loading, worst.reshape(-1)


def solution(mesh):
    return jax.shard_map(
        body,
        mesh=mesh,
        in_specs=(
            P("line", "bus"),
            P(),
            P("line", "bus"),
            P("line", "bus"),
            P("line", "bus", None, None),
            P("line"),
        ),
        out_specs=(P("bus", "line"), P("line")),
        check_vma=False,
    )
```

```python
import functools

import jax
import jax.numpy as jnp
from jax import lax
from jax.experimental import pallas as pl
from jax.experimental.pallas import tpu as pltpu
from jax.sharding import PartitionSpec as P

MESH = pl.DeviceIdType.MESH
F32 = jnp.float32
BF16 = jnp.bfloat16

LINES = 8
BUSES = 16
RING = 4
BUS_DEV = 4480
SCEN_DEV = 64
SITE_DEV = 4096
PER = 256
ROWS = (48, 32)
ROWS_ALL = 80
DIGITS = 32
SENT = (40, 32)
CHUNKS = SITE_DEV // 128
ZONES = 7
ZB = 640
LZ = 11
ZL = 512
SLOTS = 3
HALF = 256
T = 2 * LZ
NT = (((1,), (1,)), ((), ()))
LAG = (4, 8, 12, 16)
GATHERS = ((0, 0, 3), (0, 3, 2), (0, 5, 1), (0, 6, 1), (1, 0, 7))
SHARES = (4, 8, 10, 12)


def iota(shape, dim):
    return lax.broadcasted_iota(jnp.int32, shape, dim).astype(F32)


def kernel(
    count_hbm, zone_hbm, values_hbm, bus_hbm, blocks_hbm, rating_ref,
    load_hbm, worst_ref,
    live_ref, slot_ref, ids, grp, hi, lo, raw, xa, g01, pre, bt, lhs, sv0, sv1, rv0, rv1, blk, inj0, inj1,
    flows, ra, rb, sa, rc, rd, load_ref, wl, wr,
    in_sem, blk_sem, xs_sem, xr_sem, gs_sem, gr_sem, fs_sem, fr_sem, ws_sem, wr_sem, out_sem,
):
    line = lax.axis_index("line")
    bus = lax.axis_index("bus")
    y, core = line // 2, line % 2
    x, z = bus // RING, bus % RING
    up = ((y + 1) % RING) * 2 + core
    down = ((y + 3) % RING) * 2 + core
    sib = y * 2 + (1 - core)
    x1, x2, x3 = (x + 1) % RING, (x + 2) % RING, (x + 3) % RING
    z1, z2, z3 = (z + 1) % RING, (z + 2) % RING, (z + 3) % RING

    barrier = pltpu.get_barrier_semaphore()
    for j in range(1, BUSES):
        pl.semaphore_signal(barrier, inc=1, device_id=(line, (bus + j) % BUSES), device_id_type=MESH)
    for other in (up, down, sib):
        pl.semaphore_signal(barrier, inc=1, device_id=(other, bus), device_id_type=MESH)

    ids_copy = pltpu.make_async_copy(bus_hbm.at[pl.ds(bus * CHUNKS, CHUNKS)], ids, in_sem.at[0])
    ids_copy.start()
    val_copies = [
        pltpu.make_async_copy(values_hbm.at[pl.ds(16 * q, 16)], raw.at[pl.ds(row, 16)], in_sem.at[1 + q])
        for q, row in enumerate((0, 48, 16, 64))
    ]
    for copy in val_copies:
        copy.start()
    small_copies = [
        pltpu.make_async_copy(count_hbm, live_ref, in_sem.at[5]),
        pltpu.make_async_copy(zone_hbm, slot_ref, in_sem.at[6]),
    ]
    for copy in small_copies:
        copy.start()

    def block_copy(zone, slot):
        return pltpu.make_async_copy(
            blocks_hbm.at[zone, slot], blk.at[zone, :, pl.ds(slot * ZB, ZB)], blk_sem.at[zone, slot]
        )

    def start_blocks(zone, _):
        for slot in range(SLOTS):
            block_copy(zone, slot).start()
        return 0

    lax.fori_loop(0, LZ, start_blocks, 0)

    inj0[ZONES] = jnp.zeros((HALF, ZB), BF16)
    inj1[ZONES] = jnp.zeros((HALF, ZB), BF16)
    wl[...] = jnp.zeros_like(wl)
    ids_copy.wait()
    bus_ids = ids[...]
    group = jnp.zeros_like(bus_ids)
    for g in range(1, BUSES):
        group = group + (bus_ids >= g * BUS_DEV).astype(jnp.int32)
    offset = bus_ids - group * BUS_DEV
    grp[...] = group.astype(F32)
    hi[...] = (offset >> 8).astype(F32)
    lo[...] = (offset & 255).astype(F32)

    sub16 = iota((16, 128), 0)

    def lanes(c, width=128):
        return pl.ds(pl.multiple_of(c * width, width), width)

    def mark(c, _):
        row = grp[pl.ds(c, 1), :]
        g01[pl.ds(pl.multiple_of(c * 16, 16), 16), :] = jnp.where(row == sub16, 1.0, 0.0).astype(BF16)
        digits = jnp.where(sub16 == 0, hi[pl.ds(c, 1), :], jnp.where(sub16 == 1, lo[pl.ds(c, 1), :], 0.0))
        xa[pl.ds(DIGITS, 16), lanes(c)] = digits.astype(BF16)
        return 0

    lax.fori_loop(0, CHUNKS, mark, 0)
    ahead = lax.broadcasted_iota(jnp.int32, (128, 256), 0)
    place = lax.broadcasted_iota(jnp.int32, (128, 256), 1)
    steps = jnp.where((ahead <= place) | (place >= 128), 1.0, 0.0).astype(BF16)
    pre[...] = jnp.dot(g01[...], steps, preferred_element_type=F32)
    sub256 = iota((256, 128), 0)

    def rank(c, run):
        rows = pl.ds(pl.multiple_of(c * 16, 16), 16)
        counted = g01[rows, :].astype(F32) * (pre[rows, pl.ds(0, 128)] + run)
        position = jnp.sum(counted, axis=0, keepdims=True) - 1.0
        bt[:, lanes(c)] = jnp.where(position == sub256, 1.0, 0.0).astype(BF16)
        return run + pre[rows, pl.ds(128, 128)]

    lax.fori_loop(0, CHUNKS, rank, jnp.zeros((16, 128), F32))
    for copy in val_copies:
        copy.wait()

    def narrow(c, _):
        xa[pl.ds(0, 32), lanes(c)] = raw[pl.ds(0, 32), lanes(c)].astype(BF16)
        xa[pl.ds(48, 32), lanes(c)] = raw[pl.ds(48, 32), lanes(c)].astype(BF16)
        return 0

    lax.fori_loop(0, CHUNKS, narrow, 0)

    sv, rv = (sv0, sv1), (rv0, rv1)

    def chosen(row, value, vals):
        mask = jnp.where(jnp.broadcast_to(row, (16, row.shape[1])) == value, 1.0, 0.0).astype(BF16)
        return vals * jnp.concatenate([mask] * (vals.shape[0] // 16), axis=0)

    def pack(half):
        rows = ROWS[half]
        first = half * ROWS[0]
        for batch in range(2):
            owners = [(bus + batch * 8 + i + 1) % BUSES for i in range(8)]
            owners_f = [o.astype(F32) for o in owners]

            def pick(c, _):
                row = grp[pl.ds(c, 1), :]
                vals = xa[pl.ds(first, rows), lanes(c)]
                for i in range(8):
                    lhs[pl.ds(i * rows, rows), lanes(c)] = chosen(row, owners_f[i], vals)
                return 0

            lax.fori_loop(0, CHUNKS, pick, 0)
            packed = lax.dot_general(
                lhs[pl.ds(0, 8 * rows), :], bt[...], NT, preferred_element_type=F32
            ).astype(BF16)
            if half == 0 and batch == 0:
                pl.semaphore_wait(barrier, BUSES - 1 + 3)
            for i in range(8):
                j = batch * 8 + i
                if j < BUSES - 1:
                    sv[half][j] = packed[i * rows:(i + 1) * rows]
                    pltpu.make_async_remote_copy(
                        sv[half].at[j, pl.ds(0, SENT[half])], rv[half].at[bus, pl.ds(0, SENT[half])], xs_sem.at[half, j], xr_sem.at[half, bus],
                        device_id=(line, owners[i]), device_id_type=MESH,
                    ).start()
                else:
                    rv[half][bus] = packed[i * rows:(i + 1) * rows]

    def received(half):
        for j in range(1, BUSES):
            src = (bus + j) % BUSES
            rows = rv[half].at[src, pl.ds(0, SENT[half])]
            pltpu.make_async_copy(rows, rows, xr_sem.at[half, src]).wait()

    def low_digit(k, _):
        row = rv0[k, pl.ds(DIGITS, 8), :].astype(F32)[1:2]
        bt[:, lanes(k, 256)] = jnp.where(row == iota((256, 256), 0), 1.0, 0.0).astype(BF16)
        return 0

    def spread(half, inj, after):
        for part in range(2):

            def high_digit(k, _):
                vals = rv[half][k, pl.ds(0, 32), :]
                row = rv0[k, pl.ds(DIGITS, 8), :].astype(F32)[0:1]
                for i in range(9):
                    lhs[pl.ds(i * 32, 32), lanes(k, 256)] = chosen(row, float(part * 9 + i), vals)
                return 0

            lax.fori_loop(0, BUSES, high_digit, 0)
            sums = lax.dot_general(
                lhs[pl.ds(0, 288), :], bt[...], NT, preferred_element_type=F32
            ).astype(BF16)
            for i in range(9):
                for t in range(2):
                    strip = 2 * (part * 9 + i) + t
                    if strip < ZONES * 5:
                        zone, lane = strip // 5, (strip % 5) * 128
                        inj[zone, pl.ds(pl.multiple_of(line * 32, 32), 32), lane:lane + 128] = sums[
                            i * 32:(i + 1) * 32, t * 128:t * 128 + 128
                        ]
            after[part]()

    def gathered(step, owner, first, count):
        half, zone, zones = GATHERS[step]
        rows = pl.ds(pl.multiple_of(owner * 32, 32) + first, count)
        return (inj1 if half else inj0).at[pl.ds(zone, zones), rows]

    def gather(step, number, owner, first, count, target):
        rows = gathered(step, owner, first, count)
        return pltpu.make_async_remote_copy(
            rows, rows, gs_sem.at[step, number], gr_sem.at[step, number],
            device_id=(target, bus), device_id_type=MESH,
        )

    def arrival(step, number, owner, first, count):
        rows = gathered(step, owner, first, count)
        return pltpu.make_async_copy(rows, rows, gr_sem.at[step, number])

    far = ((y + 2) % RING) * 2 + core
    sib_up = ((y + 1) % RING) * 2 + (1 - core)
    sib_down = ((y + 3) % RING) * 2 + (1 - core)
    sib_far = ((y + 2) % RING) * 2 + (1 - core)

    ROUTES = (
        (line, 0, 32, up),
        (line, 0, 32, down),
        (line, 0, 32, sib),
        (down, 0, 16, up),
        (down, 0, 32, sib),
        (up, 16, 16, down),
        (up, 0, 32, sib),
        (far, 0, 16, sib),
        (far, 16, 16, sib),
    )

    def route(step, number):
        return gather(step, number, *ROUTES[number])

    def gather_start(step):
        for number in range(3):
            route(step, number).start()

    def gather_relay(step):
        arrival(step, 0, down, 0, 32).wait()
        route(step, 3).start()
        route(step, 4).start()
        arrival(step, 1, up, 0, 32).wait()
        route(step, 5).start()
        route(step, 6).start()

    def gather_last(step):
        arrival(step, 3, far, 0, 16).wait()
        route(step, 7).start()
        arrival(step, 5, far, 16, 16).wait()
        route(step, 8).start()

    def gather_finish(step):
        arrival(step, 2, sib, 0, 32).wait()
        arrival(step, 4, sib_down, 0, 32).wait()
        arrival(step, 6, sib_up, 0, 32).wait()
        arrival(step, 7, sib_far, 0, 16).wait()
        arrival(step, 8, sib_far, 16, 16).wait()

    pack(0)
    pack(1)
    received(0)
    lax.fori_loop(0, BUSES, low_digit, 0)
    early = range(1, len(GATHERS) - 1)
    late = len(GATHERS) - 1

    def each(stage, steps):
        for step in steps:
            stage(step)

    spread(0, inj0, (lambda: gather_start(0), lambda: each(gather_start, early)))
    received(1)
    spread(1, inj1, (lambda: gather_relay(0), lambda: each(gather_relay, early)))
    gather_start(late)
    each(gather_last, range(late))
    each(gather_finish, range(late))
    for copy in small_copies:
        copy.wait()

    A, B = pl.ds(0, 256), pl.ds(256, 256)
    L, R = pl.ds(0, 128), pl.ds(128, 128)
    LO, HI = pl.ds(0, 2), pl.ds(2, 2)
    ALL = pl.ds(0, 4)

    def push(src, dst, t, step, device):
        pltpu.make_async_remote_copy(
            src, dst, fs_sem.at[t, step], fr_sem.at[t, step],
            device_id=(line, device), device_id_type=MESH,
        ).start()

    xp, xm, zp, zm = x1 * RING + z, x3 * RING + z, x * RING + z1, x * RING + z3

    def produce(t, zone, inj):
        for slot in range(SLOTS):
            @pl.when(t < LZ)
            def _():
                block_copy(zone, slot).wait()
        live = live_ref[0, zone]
        pieces = []
        for slot in range(SLOTS):
            at = jnp.where(slot < live, slot_ref[slot, zone], ZONES)
            pieces.append(inj[at])
        out = lax.dot_general(
            jnp.concatenate(pieces, axis=1), blk[zone], NT, preferred_element_type=F32
        ).astype(BF16)
        flows[t] = out.reshape(RING, RING, 16, ZL)
        push(flows.at[t, x2, LO, :, A], ra.at[t, 0], t, 0, xp)
        push(flows.at[t, x2, HI, :, A], ra.at[t, 1], t, 0, xm)
        push(flows.at[t, LO, z2, :, B], ra.at[t, 2], t, 0, zp)
        push(flows.at[t, HI, z2, :, B], ra.at[t, 3], t, 0, zm)

    def arrived(buf, t, step):
        pltpu.make_async_copy(buf.at[t], buf.at[t], fr_sem.at[t, step]).wait()

    def add(a, b):
        return (a.astype(F32) + b.astype(F32)).astype(BF16)

    def first_b(t):
        arrived(ra, t, 0)
        sums = (
            add(flows[t, x1, LO, :, A], ra[t, 0]),
            add(flows[t, x3, HI, :, A], ra[t, 1]),
            add(flows[t, LO, z1, :, B], ra[t, 2]),
            add(flows[t, HI, z3, :, B], ra[t, 3]),
        )
        flows[t, x1, LO, :, A] = sums[0]
        flows[t, x3, HI, :, A] = sums[1]
        flows[t, LO, z1, :, B] = sums[2]
        flows[t, HI, z3, :, B] = sums[3]
        push(flows.at[t, x1, ALL, :, A], rb.at[t, 0], t, 1, xp)
        push(flows.at[t, x3, ALL, :, A], rb.at[t, 1], t, 1, xm)
        push(flows.at[t, ALL, z1, :, B], rb.at[t, 2], t, 1, zp)
        push(flows.at[t, ALL, z3, :, B], rb.at[t, 3], t, 1, zm)

    def add3(a, b, c):
        return a.astype(F32) + b.astype(F32) + c.astype(F32)

    def second_a(t):
        arrived(rb, t, 1)
        sums = (
            add3(flows[t, x, ALL, :, A], rb[t, 0], rb[t, 1]).astype(BF16),
            add3(flows[t, ALL, z, :, B], rb[t, 2], rb[t, 3]).astype(BF16),
        )
        sa[t, 0] = sums[0]
        sa[t, 1] = sums[1]
        push(sa.at[t, 0, z2, :, L], rc.at[t, 0], t, 2, zp)
        push(sa.at[t, 0, z2, :, R], rc.at[t, 1], t, 2, zm)
        push(sa.at[t, 1, x2, :, L], rc.at[t, 2], t, 2, xp)
        push(sa.at[t, 1, x2, :, R], rc.at[t, 3], t, 2, xm)

    def second_b(t):
        arrived(rc, t, 2)
        sums = (
            add(sa[t, 0, z1, :, L], rc[t, 0]),
            add(sa[t, 0, z3, :, R], rc[t, 1]),
            add(sa[t, 1, x1, :, L], rc[t, 2]),
            add(sa[t, 1, x3, :, R], rc[t, 3]),
        )
        sa[t, 0, z1, :, L] = sums[0]
        sa[t, 0, z3, :, R] = sums[1]
        sa[t, 1, x1, :, L] = sums[2]
        sa[t, 1, x3, :, R] = sums[3]
        push(sa.at[t, 0, z1], rd.at[t, 0], t, 3, zp)
        push(sa.at[t, 0, z3], rd.at[t, 1], t, 3, zm)
        push(sa.at[t, 1, x1], rd.at[t, 2], t, 3, xp)
        push(sa.at[t, 1, x3], rd.at[t, 3], t, 3, xm)

    def leave(t, zone, half):
        part = (pl.ds(pl.multiple_of(half * 16, 16), 16), lanes(zone, ZL))
        return pltpu.make_async_copy(load_ref.at[part], load_hbm.at[part], out_sem.at[t])

    def finish(t, zone, half):
        arrived(rd, t, 3)
        ratings = jnp.concatenate([rating_ref[pl.ds(zone * 4 + i, 1), :] for i in range(4)], axis=1)
        flow = jnp.concatenate(
            [add3(sa[t, 0, z], rd[t, 0], rd[t, 1]), add3(sa[t, 1, x], rd[t, 2], rd[t, 3])], axis=1
        )
        loading = flow / ratings
        load_ref[pl.ds(pl.multiple_of(half * 16, 16), 16), lanes(zone, ZL)] = loading
        leave(t, zone, half).start()
        top = jnp.max(jnp.abs(loading), axis=0, keepdims=True)
        for i in range(4):
            row = pl.ds(zone * 4 + i, 1)
            wl[row, :] = jnp.maximum(wl[row, :], top[:, i * 128:(i + 1) * 128])
        for step, buf in enumerate((ra, rb, rc, rd)):
            pltpu.make_async_copy(buf.at[t], buf.at[t], fs_sem.at[t, step]).wait()

    parts = [pl.ds(first * 4, (last - first) * 4) for first, last in zip((0, *SHARES), SHARES)]

    def share(part):
        for j in range(1, BUSES):
            pltpu.make_async_remote_copy(
                wl.at[parts[part]], wr.at[bus, parts[part]], ws_sem.at[part, j], wr_sem.at[part, bus],
                device_id=(line, (bus + j) % BUSES), device_id_type=MESH,
            ).start()

    def stages(t):
        d1, d2, d3, d4 = LAG

        def when(lag, stage):
            @pl.when((t >= lag) & (t < T + lag))
            def _():
                stage(t - lag)

        when(d1, first_b)
        when(d2, second_a)
        when(d3, second_b)

        @pl.when((t >= d4) & (t < T + d4))
        def _():
            finish(t - d4, (t - d4) % LZ, (t - d4) // LZ)

        for part in range(len(parts) - 1):
            @pl.when(t == d4 + LZ + SHARES[part] - 1)
            def _(part=part):
                share(part)

    def first_half(t, _):
        produce(t, t, inj0)

        @pl.when(t == 4)
        def _():
            gather_relay(late)

        @pl.when(t == 8)
        def _():
            gather_last(late)

        stages(t)
        return 0

    def second_half(t, _):
        produce(t, t - LZ, inj1)
        stages(t)
        return 0

    def drain(t, _):
        stages(t)
        return 0

    lax.fori_loop(0, LZ, first_half, 0)
    gather_finish(late)
    lax.fori_loop(LZ, T, second_half, 0)
    lax.fori_loop(T, T + LAG[3], drain, 0)

    share(len(parts) - 1)
    for step in range(len(GATHERS)):
        for number in range(len(ROUTES)):
            route(step, number).wait_send()
    for half in range(2):
        for j in range(BUSES - 1):
            rows = sv[half].at[j, pl.ds(0, SENT[half])]
            pltpu.make_async_copy(rows, rows, xs_sem.at[half, j]).wait()

    def gone(t, _):
        leave(t, t % LZ, t // LZ).wait()
        return 0

    lax.fori_loop(0, T, gone, 0)
    best = wl[...]
    for part in range(len(parts)):
        for j in range(1, BUSES):
            src = wr.at[(bus + j) % BUSES, parts[part]]
            pltpu.make_async_copy(src, src, wr_sem.at[part, (bus + j) % BUSES]).wait()
    for j in range(1, BUSES):
        best = jnp.maximum(best, wr[(bus + j) % BUSES])
    worst_ref[...] = best[0:LZ * 4]
    for part in range(len(parts)):
        for j in range(1, BUSES):
            src = wl.at[parts[part]]
            pltpu.make_async_copy(src, src, ws_sem.at[part, j]).wait()


def hand_over(load_in, worst_in, load_ref, worst_ref):
    load_ref[...] = load_in[...]
    worst_ref[...] = worst_in[...]


def body(site_values, site_bus, block_count, block_zone, ptdf_blocks, rating):
    hbm = pl.BlockSpec(memory_space=pl.ANY)
    vmem = pl.BlockSpec(memory_space=pltpu.VMEM)
    dma = pltpu.SemaphoreType.DMA
    loading, worst = pl.pallas_call(
        kernel,
        out_shape=(
            jax.ShapeDtypeStruct((32, LZ * ZL), F32),
            jax.ShapeDtypeStruct((LZ * 4, 128), F32),
        ),
        in_specs=[hbm, hbm, hbm, hbm, hbm, vmem],
        out_specs=(hbm, vmem),
        scratch_shapes=[
            pltpu.SMEM((1, LZ), jnp.int32),
            pltpu.SMEM((SLOTS, LZ), jnp.int32),
            pltpu.VMEM((CHUNKS, 128), jnp.int32),
            pltpu.VMEM((CHUNKS, 128), F32),
            pltpu.VMEM((CHUNKS, 128), F32),
            pltpu.VMEM((CHUNKS, 128), F32),
            pltpu.VMEM((ROWS_ALL, SITE_DEV), F32),
            pltpu.VMEM((ROWS_ALL, SITE_DEV), BF16),
            pltpu.VMEM((CHUNKS * 16, 128), BF16),
            pltpu.VMEM((CHUNKS * 16, 256), F32),
            pltpu.VMEM((256, SITE_DEV), BF16),
            pltpu.VMEM((384, SITE_DEV), BF16),
            pltpu.VMEM((BUSES - 1, ROWS[0], PER), BF16),
            pltpu.VMEM((BUSES - 1, ROWS[1], PER), BF16),
            pltpu.VMEM((BUSES, ROWS[0], PER), BF16),
            pltpu.VMEM((BUSES, ROWS[1], PER), BF16),
            pltpu.VMEM((LZ, ZL, SLOTS * ZB), BF16),
            pltpu.VMEM((ZONES + 1, HALF, ZB), BF16),
            pltpu.VMEM((ZONES + 1, HALF, ZB), BF16),
            pltpu.VMEM((T, RING, RING, 16, ZL), BF16),
            pltpu.VMEM((T, 4, 2, 16, 256), BF16),
            pltpu.VMEM((T, 4, 4, 16, 256), BF16),
            pltpu.VMEM((T, 2, 4, 16, 256), BF16),
            pltpu.VMEM((T, 4, 16, 128), BF16),
            pltpu.VMEM((T, 4, 16, 256), BF16),
            pltpu.VMEM((32, LZ * ZL), F32),
            pltpu.VMEM((48, 128), F32),
            pltpu.VMEM((BUSES, 48, 128), F32),
            dma((7,)),
            dma((LZ, SLOTS)),
            dma((2, BUSES)),
            dma((2, BUSES)),
            dma((len(GATHERS), 9)),
            dma((len(GATHERS), 9)),
            dma((T, 4)),
            dma((T, 4)),
            dma((len(SHARES), BUSES)),
            dma((len(SHARES), BUSES)),
            dma((T,)),
        ],
        compiler_params=pltpu.CompilerParams(
            collective_id=0, has_side_effects=True, vmem_limit_bytes=62 * 1024 * 1024
        ),
        name="screen",
    )(
        block_count.T, block_zone.T, site_values, site_bus.reshape(-1, 128), ptdf_blocks,
        rating.reshape(-1, 128),
    )
    loading, worst = pl.pallas_call(
        hand_over,
        out_shape=(
            jax.ShapeDtypeStruct((32, LZ * ZL), F32),
            jax.ShapeDtypeStruct((LZ * 4, 128), F32),
        ),
        in_specs=[vmem, vmem],
        out_specs=(vmem, vmem),
        name="hand_over",
    )(loading, worst)
    return loading, worst.reshape(-1)


def solution(mesh):
    return jax.shard_map(
        body,
        mesh=mesh,
        in_specs=(
            P("line", "bus"),
            P(),
            P("line", "bus"),
            P("line", "bus"),
            P("line", "bus", None, None),
            P("line"),
        ),
        out_specs=(P("bus", "line"), P("line")),
        check_vma=False,
    )
```
